512 devices in a mesh: flow: 8 (over y, core), cross: 64 (over x, z).
Axes of the slice: x: 4, y: 4, z: 16, core: 2. Of those that a mesh axis runs over, the one named last changes fastest.
Arguments:
- source: float32 [16, 64, 131072], P('flow', None, 'cross'), may hold values from -6 to 6
- cotangent: float32 [16, 64, 131072], P('flow', None, 'cross'), may hold values from -6 to 6
- flux: float32 [16, 131072], P('flow', 'cross'), may hold values from 0.3 to 1
- pore_mask: int32 [16, 131072], P('flow', 'cross'), may hold values 0 or 1
- upwind: int32 [16, 131072], P('flow', 'cross'), may hold values 0 or 1
- side_link: int32 [16, 131072], P('flow', 'cross'), may hold values from 0 to 159
- local_inverse: float32 [64, 64], replicated, may hold values from -0.75 to 0.75
- flow_lift: float32 [64, 16], replicated, may hold values from -2 to 2
- side_lift: float32 [64, 16], replicated, may hold values from -2 to 2
- flow_trace: float32 [16, 64], replicated, may hold values from -0.75 to 0.75
- side_trace: float32 [16, 64], replicated, may hold values from -0.75 to 0.75
Outputs:
- concentration: float32 [16, 64, 131072], P('flow', None, 'cross')
- sensitivity: float32 [16, 64, 131072], P('flow', None, 'cross')
The draws below stay inside these ranges and needn't reach their ends.
Inputs may be any that keep to these rules, and one draw needn't show every extreme that they name: `side_link`: entries 0 to 15 name the left cross neighbour's edge elements, 16 to 143 the tile's own slots, the rest the right neighbour's edge elements.
All inputs are finite; a program needn't handle non-finite values. No bound on the sum of `pore_mask` or of `upwind` on one device may be relied on, other than what follows from the above.
Results may differ from the reference program's by a relative error of at most 0.00012.
Values sent between devices are 32-bit elements; how exact they have to be, the bound alone decides.
A program may use at most 64 MiB of HBM per device.

```python
import math
import jax
import jax.numpy as jnp
from jax import lax

NODES = 64
FACE = 16
TILE = 128
HALO = 16
TILES = 16
LEVELS = 16
ELEMS = 131072
N_CROSS = 64


def with_ends(values, own_key, least, largest):
    spot = [jax.random.randint(jax.random.fold_in(own_key, axis), (), 0, length) for axis, length in enumerate(values.shape)]
    main_axis = values.shape.index(max(values.shape))
    beside = spot[:main_axis] + [(spot[main_axis] + 1) % values.shape[main_axis]] + spot[main_axis + 1:]
    return values.at[tuple(spot)].set(least).at[tuple(beside)].set(largest)


def block_levels(own_key, extent, shards, smallest, high):
    factor_of = 1.0
    for axis_at, shards_of in shards:
        steps = jax.random.uniform(jax.random.fold_in(jax.random.fold_in(own_key, 6), axis_at), (shards_of,), jnp.float32, smallest / len(shards), high / len(shards))
        factor_of = factor_of * jnp.repeat(jnp.exp(steps), extent[axis_at] // shards_of).reshape((-1,) + (1,) * (len(extent) - 1 - axis_at))
    return factor_of


def centred(stream_key, extent, spread, reach, shards=(), kind=jnp.bfloat16):
    drawn = jax.random.normal(stream_key, extent, jnp.float32) * spread
    if len(shards) > 0:
        drawn = block_levels(stream_key, extent, shards, -0.22, 0.18) * drawn
    return jnp.clip(drawn, min=-reach, max=reach).astype(kind)


def setup_inputs(seed: int = 0) -> dict:
    streams_of = jax.random.split(jax.random.key(seed), 12)
    return {
        "source": centred(streams_of[0], (LEVELS, NODES, ELEMS), 1.0, 6.0, ((0, 8), (2, 64)), jnp.float32),
        "cotangent": centred(streams_of[1], (LEVELS, NODES, ELEMS), 1.0, 6.0, ((0, 8), (2, 64)), jnp.float32),
        "flux": jnp.clip(jnp.exp(math.log(1.0) - 1.2039728 * jax.random.uniform(streams_of[2], (LEVELS, ELEMS), jnp.float32) ** block_levels(streams_of[2], (LEVELS, ELEMS), ((0, 8), (1, 64)), -0.2, 0.2)), 0.3, 1.0),
        "pore_mask": with_ends((jax.random.randint(streams_of[3], (LEVELS, ELEMS), 0, 4) < 3).astype(jnp.int32), jax.random.fold_in(streams_of[3], 1), 0, 1),
        "upwind": with_ends((jax.random.randint(streams_of[4], (LEVELS, ELEMS), 0, 2) < 1).astype(jnp.int32), jax.random.fold_in(streams_of[4], 1), 0, 1),
        "side_link": with_ends(jax.random.randint(streams_of[5], (LEVELS, ELEMS), 0, TILE + 2 * HALO), jax.random.fold_in(streams_of[5], 1), 0, (TILE + 2 * HALO) - 1).astype(jnp.int32),
        "local_inverse": centred(streams_of[6], (NODES, NODES), NODES ** -0.5, 0.75, (), jnp.float32),
        "flow_lift": centred(streams_of[7], (NODES, FACE), 8 ** -0.5, 2.0, (), jnp.float32),
        "side_lift": centred(streams_of[8], (NODES, FACE), 8 ** -0.5, 2.0, (), jnp.float32),
        "flow_trace": centred(streams_of[9], (FACE, NODES), NODES ** -0.5, 0.75, (), jnp.float32),
        "side_trace": centred(streams_of[10], (FACE, NODES), NODES ** -0.5, 0.75, (), jnp.float32),
    }


def extend_row(side_rows):
    grid = side_rows.reshape(FACE, N_CROSS, TILES, TILE)
    zero = jnp.zeros((FACE, 1, TILES, HALO), side_rows.dtype)
    left = jnp.concatenate([zero, grid[:, :-1, :, TILE - HALO:]], axis=1)
    right = jnp.concatenate([grid[:, 1:, :, :HALO], zero], axis=1)
    return jnp.concatenate([left, grid, right], axis=3)

def reference(source, cotangent, flux, pore_mask, upwind, side_link, local_inverse, flow_lift, side_lift, flow_trace, side_trace):
    high = lax.Precision.HIGHEST

    def forward(src):
        base = jnp.einsum('mn,lne->lme', local_inverse, src, precision=high)

        def level(carry, inputs):
            flow_in, side_rows = carry
            based, coeff, live, inflow, links = inputs
            extended = extend_row(side_rows)
            picked = jnp.take_along_axis(extended, links.reshape(1, N_CROSS, TILES, TILE), axis=3)
            side_in = picked.reshape(FACE, -1) * inflow.astype(src.dtype)
            lifted = jnp.dot(flow_lift, flow_in, precision=high) + jnp.dot(side_lift, side_in, precision=high)
            conc = live.astype(src.dtype) * (based + coeff * lifted)
            return ((jnp.dot(flow_trace, conc, precision=high), jnp.dot(side_trace, conc, precision=high)), conc)
        zero = jnp.zeros((FACE, src.shape[2]), src.dtype)
        unused, concs = lax.scan(level, (zero, zero), (base, flux, pore_mask, upwind, side_link))
        return concs
    concentration, pullback = jax.vjp(forward, source)
    sensitivity = pullback(cotangent)[0]
    return (concentration, sensitivity)
```

```python
import jax
import jax.numpy as jnp
from jax import lax
from jax.experimental import pallas as pl
from jax.experimental.pallas import tpu as pltpu
from jax.sharding import PartitionSpec as P

FACE = 16
TILE = 128
HALO = 16
LEVELS_HERE = 2
GROUP = 4
HALF = TILE // 2
BOTH = 2 * FACE
NEAR = 3 * FACE

HIGH = lax.Precision.HIGHEST
F32 = jnp.float32
BF16 = jnp.bfloat16
MESH = pl.DeviceIdType.MESH


def halves(value):
    high = value.astype(BF16)
    low = (value - high.astype(F32)).astype(BF16)
    return high, low


def stacked(value):
    high, low = halves(value)
    return jnp.concatenate([high, low, high], axis=0)


def product(left, right):
    return jnp.dot(left, right, preferred_element_type=F32)


def cross_product(left, right):
    return lax.dot_general(left, right, (((1,), (1,)), ((), ())), preferred_element_type=F32)


def widened(weight, wide, target):
    depth = weight.shape[1]
    high = weight.astype(BF16).astype(F32)
    wide[0 : weight.shape[0], 0:depth] = high
    wide[0 : weight.shape[0], depth : 2 * depth] = high
    wide[0 : weight.shape[0], 2 * depth : 3 * depth] = weight - high
    target[...] = wide[0 : weight.shape[0], 0 : 3 * depth].astype(BF16)


def kernel(
    source,
    cotangent,
    flux,
    pore_mask,
    upwind,
    side_link,
    local_inverse,
    flow_lift,
    side_lift,
    flow_trace,
    side_trace,
    concentration,
    sensitivity,
    field,
    lead,
    scale,
    pick,
    pick_beside,
    pick_next,
    kept,
    late,
    main_in,
    main_out,
    near_out,
    near_left,
    near_right,
    far_left,
    far_right,
    fix_out,
    fix_left,
    fix_right,
    fact_out,
    fact_left,
    fact_right,
    fact_next,
    start_out,
    start_left,
    start_right,
    lift,
    wide,
    local_weight,
    chain_weight,
    out_weight,
    field_sem,
    done_sem,
    main_sem,
    near_sem,
    far_sem,
    fix_sem,
    fact_sem,
    next_sem,
    start_sem,
):
    flow_count = lax.axis_size("flow")
    cross_count = lax.axis_size("cross")
    place = lax.axis_index("flow")
    block = lax.axis_index("cross")
    pieces = main_in.shape[1]
    whole_width = main_in.shape[3]
    width = whole_width - TILE
    nodes = field.shape[2]
    inputs = (source, cotangent)
    results = (concentration, sensitivity)
    is_first = (place == 0, place == flow_count - 1)
    is_last = (place == flow_count - 1, place == 0)
    downstream = (place + 1, place - 1)
    below, above = place > 0, place < flow_count - 1

    def beside(steps):
        return lax.rem(block + cross_count + steps, cross_count)

    def loaded(sweep):
        return pltpu.make_async_copy(inputs[sweep], field.at[sweep], field_sem.at[sweep])

    loaded(0).start()
    loaded(1).start()

    barrier = pltpu.get_barrier_semaphore()

    def greet(flow_at, steps):
        pl.semaphore_signal(
            barrier, inc=1, device_id=(flow_at, beside(steps)), device_id_type=MESH
        )

    greet(place, -1)
    greet(place, 1)

    @pl.when(below)
    def _():
        for steps in range(-2, 3):
            greet(place - 1, steps)

    @pl.when(above)
    def _():
        for steps in range(-2, 3):
            greet(place + 1, steps)

    inverse = local_inverse[...]
    lift[:, 0:FACE] = flow_lift[...]
    lift[:, FACE:BOTH] = side_lift[...]
    lifts = lift[...]
    trace = jnp.concatenate([flow_trace[...], side_trace[...]], axis=0)
    traced_inverse = jnp.dot(trace, inverse, precision=HIGH, preferred_element_type=F32)
    traced_lift = jnp.dot(trace, lifts, precision=HIGH, preferred_element_type=F32)
    widened(jnp.concatenate([inverse, traced_inverse], axis=0), wide, local_weight.at[0])
    widened(jnp.concatenate([inverse.T, lifts.T], axis=0), wide, local_weight.at[1])
    widened(traced_lift, wide, chain_weight.at[0])
    widened(traced_lift.T, wide, chain_weight.at[1])
    widened(lifts, wide, out_weight.at[0])
    widened(traced_inverse.T, wide, out_weight.at[1])

    def lanes(rows):
        return lax.broadcasted_iota(jnp.int32, (rows, TILE), 1)

    def packed(value):
        lane = lanes(value.shape[0])
        edge = jnp.zeros(lane.shape, F32)
        for at in range(GROUP):
            tile = value[:, at * TILE : (at + 1) * TILE]
            start = at * HALO
            tail = pltpu.roll(tile, (start + HALO) % TILE, 1)
            head = pltpu.roll(tile, (start + HALF) % TILE, 1)
            edge = jnp.where((lane >= start) & (lane < start + HALO), tail, edge)
            edge = jnp.where((lane >= start + HALF) & (lane < start + HALF + HALO), head, edge)
        return edge

    def unpacked(edge, at):
        lane = lanes(edge.shape[0])
        start = at * HALO
        head = pltpu.roll(edge, (TILE - HALF - start) % TILE, 1)
        tail = pltpu.roll(edge, (TILE - HALO - start) % TILE, 1)
        return jnp.where(lane < HALO, head, jnp.where(lane >= TILE - HALO, tail, 0.0))

    def is_open(reach):
        return (
            (block >= reach).astype(jnp.int32),
            (block < cross_count - reach).astype(jnp.int32),
        )

    def inward(from_left, from_right, reach=1):
        lane = lanes(from_left.shape[0])
        opened = jnp.where(lane < HALF, *is_open(reach))
        return jnp.where(opened > 0, jnp.where(lane < HALF, from_left, from_right), 0.0)

    def homeward(from_left, from_right, reach=1):
        lane = lanes(from_left.shape[0])
        opened = jnp.where(lane < HALF, *is_open(reach)[::-1])
        return jnp.where(opened > 0, jnp.where(lane < HALF, from_right, from_left), 0.0)

    def columns_of(piece):
        return pl.ds(pl.multiple_of(piece * width, width), width)

    def live(level, piece):
        return pore_mask[level : level + 1, columns_of(piece)].astype(F32)

    def codes(level, piece):
        cols = columns_of(piece)
        inflow = upwind[level : level + 1, cols]
        return jnp.where(inflow != 0, side_link[level : level + 1, cols], -1)

    def gather_facts(piece, carry):
        for level in range(LEVELS_HERE):
            cols = columns_of(piece)
            scale[level, piece, :, 0:width] = live(level, piece) * flux[level : level + 1, cols]
        rows = jnp.concatenate(
            [
                scale[0, piece, :, 0:width],
                codes(0, piece).astype(F32),
                jnp.zeros((6, width), F32),
            ],
            axis=0,
        )
        fact_out[piece] = packed(rows)
        return carry

    lax.fori_loop(0, pieces, gather_facts, 0)

    def send(src, dst, send_sem, recv_sem, flow_at, steps):
        return pltpu.make_async_remote_copy(
            src_ref=src,
            dst_ref=dst,
            send_sem=send_sem,
            recv_sem=recv_sem,
            device_id=(flow_at, beside(steps)),
            device_id_type=MESH,
        )

    def pair(src, at_left, at_right, sem, flow_at, reach=1):
        return (
            send(src, at_left, sem(0), sem(1), flow_at, reach),
            send(src, at_right, sem(2), sem(3), flow_at, -reach),
        )

    def fact_copies():
        return pair(fact_out, fact_left, fact_right, lambda n: fact_sem.at[n], place)

    def next_copy():
        return send(fact_out, fact_next, next_sem.at[0], next_sem.at[1], place - 1, 0)

    def start_copies():
        return pair(start_out, start_left, start_right, lambda n: start_sem.at[n], place)

    def fix_copies(piece):
        return pair(
            fix_out.at[piece],
            fix_left.at[piece],
            fix_right.at[piece],
            lambda n: fix_sem.at[n, piece],
            place,
        )

    def wave_copies(sweep, piece):
        flow_at = downstream[sweep]
        main = send(
            main_out.at[sweep, piece],
            main_in.at[sweep, piece],
            main_sem.at[0, sweep, piece],
            main_sem.at[1, sweep, piece],
            flow_at,
            0,
        )
        near = pair(
            near_out.at[sweep, piece, pl.ds(0, NEAR)],
            near_left.at[sweep, piece],
            near_right.at[sweep, piece],
            lambda n: near_sem.at[n, sweep, piece],
            flow_at,
        )
        far = pair(
            near_out.at[sweep, piece, pl.ds(NEAR, FACE)],
            far_left.at[sweep, piece],
            far_right.at[sweep, piece],
            lambda n: far_sem.at[n, sweep, piece],
            flow_at,
            2,
        )
        return near + far + (main,)

    pl.semaphore_wait(barrier, 2 + 5 * below.astype(jnp.int32) + 5 * above.astype(jnp.int32))

    for copy in fact_copies():
        copy.start()

    @pl.when(below)
    def _():
        next_copy().start()

    def one_hot(row, depth):
        rows = lax.broadcasted_iota(jnp.int32, (depth, TILE), 0)
        return jnp.where(rows == row, 1.0, 0.0).astype(BF16)

    def build_pick(piece, carry):
        for level in range(LEVELS_HERE):
            code = codes(level, piece)
            for at in range(GROUP):
                link = code[:, at * TILE : (at + 1) * TILE]
                row = jnp.where(
                    link < HALO,
                    link + (TILE + at * HALO),
                    jnp.where(
                        link < HALO + TILE, link - HALO, link + (HALF + at * HALO - HALO)
                    ),
                )
                row = jnp.where(link >= 0, row, -1)
                pick[level, piece * GROUP + at] = one_hot(row, 2 * TILE)
        return carry

    lax.fori_loop(0, pieces, build_pick, 0)

    def settle_facts():
        for copy in fact_copies():
            copy.wait_recv()

        @pl.when(above)
        def _():
            next_copy().wait_recv()

        @pl.when(jnp.logical_not(above))
        def _():
            fact_next[...] = jnp.zeros(fact_next.shape, F32)

        lane = lanes(1)
        start = lax.rem(lane, HALF) // HALO * HALO
        on_left = lane < HALF

        def one(piece, carry):
            facts = inward(fact_left[piece], fact_right[piece])
            scale[0, piece, :, width:whole_width] = facts[0:1]
            link = facts[1:2].astype(jnp.int32)
            low = (link >= 0) & (link < HALO)
            high = link >= HALO + TILE
            after = link - (HALO + TILE)
            left_row = jnp.where(
                high, HALF + start + after, jnp.where(low, TILE + start + link, -1)
            )
            right_row = jnp.where(
                low, start + link, jnp.where(high, TILE + HALF + start + after, -1)
            )
            pick_beside[piece] = one_hot(jnp.where(on_left, left_row, right_row), 2 * TILE)
            link = fact_next[piece][1:2].astype(jnp.int32)
            inside = (link >= HALO) & (link < HALO + TILE)
            row = jnp.where(inside, start * (TILE // HALO) + link - HALO, -1)
            pick_next[piece] = one_hot(row, width)
            return carry

        lax.fori_loop(0, pieces, one, 0)

    def prepare(sweep):
        loaded(sweep).wait()

        def one(level, piece):
            cols = columns_of(piece)
            value = product(local_weight[sweep], stacked(field[sweep, level, :, cols]))
            mask = live(level, piece)
            field[sweep, level, :, cols] = mask * value[:nodes]
            added = (mask if sweep == 0 else scale[level, piece, :, 0:width]) * value[nodes:]
            lead[sweep, level, piece, :, 0:width] = added
            if level == 0:
                lead[sweep, 0, piece, :, width:whole_width] = jnp.zeros((BOTH, TILE), F32)
                if sweep == 0:
                    start_out[piece] = packed(added[FACE:])

        def first_level(piece, carry):
            one(0, piece)
            return carry

        def second_level(piece, carry):
            one(1, piece)
            return carry

        lax.fori_loop(0, pieces, first_level, 0)
        if sweep == 0:
            for copy in start_copies():
                copy.start()
        lax.fori_loop(0, pieces, second_level, 0)

    def arrive(sweep, piece):
        @pl.when(is_first[sweep])
        def _():
            main_in[sweep, piece] = jnp.zeros((BOTH, whole_width), F32)
            near_left[sweep, piece] = jnp.zeros((NEAR, TILE), F32)
            near_right[sweep, piece] = jnp.zeros((NEAR, TILE), F32)
            far_left[sweep, piece] = jnp.zeros((FACE, TILE), F32)
            far_right[sweep, piece] = jnp.zeros((FACE, TILE), F32)

        @pl.when(jnp.logical_not(is_first[sweep]))
        def _():
            for copy in wave_copies(sweep, piece):
                copy.wait_recv()

    def leave(sweep, piece):
        for copy in wave_copies(sweep, piece):
            copy.start()

    def picked(near, beyond, one_hots):
        near_high, near_low = near
        beyond_high, beyond_low = beyond
        extended = jnp.concatenate(
            [
                jnp.concatenate([near_high, beyond_high], axis=1),
                jnp.concatenate([near_low, beyond_low], axis=1),
            ],
            axis=0,
        )
        value = product(extended, one_hots)
        return value[:FACE] + value[FACE:]

    def spread(value, one_hots):
        value = cross_product(jnp.concatenate(halves(value), axis=0), one_hots)
        return value[:FACE] + value[FACE:]

    def cut(value, at):
        return value[:, at * TILE : (at + 1) * TILE]

    def gathered(sides, halo, level, piece):
        halo = halves(halo)
        high, low = halves(sides)
        return [
            picked((cut(high, at), cut(low, at)), halo, pick[level, piece * GROUP + at])
            for at in range(GROUP)
        ]

    def scattered(sides, level, piece):
        own = []
        edge = jnp.zeros((FACE, TILE), F32)
        for at in range(GROUP):
            value = spread(cut(sides, at), pick[level, piece * GROUP + at])
            own.append(value[:, :TILE])
            edge = edge + value[:, TILE:]
        return own, edge

    def forward(piece):
        arrive(0, piece)
        main = main_in[0, piece]
        near = inward(near_left[0, piece], near_right[0, piece])
        outer = inward(far_left[0, piece], far_right[0, piece], 2)
        sides = gathered(main[FACE:, :width], near[BOTH:], 0, piece)
        sides.append(
            near[FACE:BOTH]
            + picked(halves(main[FACE:, width:]), halves(outer), pick_beside[piece])
        )
        inbound = jnp.concatenate(
            [
                jnp.concatenate([main[:FACE, :width], near[:FACE]], axis=1),
                jnp.concatenate(sides, axis=1),
            ],
            axis=0,
        )
        operand = stacked(inbound)
        kept[0, 0, piece] = operand[:, :width]
        value = lead[0, 0, piece] + scale[0, piece] * product(chain_weight[0], operand)
        sides = gathered(value[FACE:, :width], value[FACE:, width:], 1, piece)
        operand = stacked(
            jnp.concatenate([value[:FACE, :width], jnp.concatenate(sides, axis=1)], axis=0)
        )
        kept[0, 1, piece] = operand

        @pl.when(jnp.logical_not(is_last[0]))
        def _():
            value = lead[0, 1, piece, :, 0:width] + scale[1, piece, :, 0:width] * product(
                chain_weight[0], operand
            )
            edges = packed(value)
            ahead = product(jnp.concatenate(halves(value[FACE:]), axis=0), pick_next[piece])
            main_out[0, piece, :, 0:width] = value
            main_out[0, piece, :, width:whole_width] = edges
            near_out[0, piece, 0:FACE] = edges[:FACE]
            near_out[0, piece, FACE:BOTH] = ahead[:FACE] + ahead[FACE:]
            near_out[0, piece, BOTH:NEAR] = edges[FACE:]
            near_out[0, piece, NEAR : NEAR + FACE] = edges[FACE:]
            leave(0, piece)

    def adjoint(piece):
        arrive(1, piece)
        main = main_in[1, piece]
        near = homeward(near_left[1, piece], near_right[1, piece])
        outer = homeward(far_left[1, piece], far_right[1, piece], 2)
        edges = jnp.concatenate(
            [near[:FACE], main[FACE:, width:] + near[BOTH:] + outer], axis=0
        )
        behind = spread(near[FACE:BOTH], pick_next[piece])
        none = jnp.zeros((FACE, TILE), F32)
        inbound = jnp.concatenate(
            [
                cut(main, at)
                + unpacked(edges, at)
                + jnp.concatenate([none, cut(behind, at)], axis=0)
                for at in range(GROUP)
            ],
            axis=1,
        )
        operand = stacked(inbound)
        kept[1, 1, piece] = operand
        value = lead[1, 1, piece, :, 0:width] + scale[1, piece, :, 0:width] * product(
            chain_weight[1], operand
        )
        own, edge = scattered(value[FACE:], 1, piece)
        fix_out[piece] = edge
        for copy in fix_copies(piece):
            copy.start()
        inbound = jnp.concatenate(
            [
                jnp.concatenate([value[:FACE], none], axis=1),
                jnp.concatenate(own + [edge], axis=1),
            ],
            axis=0,
        )
        late[piece] = inbound[:, :width]

        @pl.when(jnp.logical_not(is_last[1]))
        def _():
            value = lead[1, 0, piece] + scale[0, piece] * product(
                chain_weight[1], stacked(inbound)
            )
            own, edge = scattered(value[FACE:, :width], 0, piece)
            around = spread(value[FACE:, width:], pick_beside[piece])
            own.append(around[:, :TILE])
            main_out[1, piece, 0:FACE] = jnp.concatenate([value[:FACE, :width], none], axis=1)
            main_out[1, piece, FACE:BOTH] = jnp.concatenate(own, axis=1)
            near_out[1, piece, 0:BOTH] = value[:, width:]
            near_out[1, piece, BOTH:NEAR] = edge
            near_out[1, piece, NEAR : NEAR + FACE] = around[:, TILE:]
            leave(1, piece)

    def written(sweep, piece):
        cols = columns_of(piece)
        return pltpu.make_async_copy(
            field.at[sweep, :, :, cols], results[sweep].at[:, :, cols], done_sem.at[sweep, piece]
        )

    def finish(sweep, piece):
        cols = columns_of(piece)
        for level in range(LEVELS_HERE):
            if sweep == 1 and level == 0:
                for copy in fix_copies(piece):
                    copy.wait_recv()
                edges = homeward(fix_left[piece], fix_right[piece])
                sides = [
                    cut(late[piece, FACE:BOTH], at) + unpacked(edges, at) for at in range(GROUP)
                ]
                operand = stacked(
                    jnp.concatenate(
                        [late[piece, 0:FACE], jnp.concatenate(sides, axis=1)], axis=0
                    )
                )
            else:
                operand = kept[sweep, level, piece]
            factor = scale[level, piece, :, 0:width] if sweep == 0 else live(level, piece)
            field[sweep, level, :, cols] += factor * product(out_weight[sweep], operand)
        written(sweep, piece).start()

    def chain(sweep):
        step = forward if sweep == 0 else adjoint
        if sweep == 0:
            for copy in start_copies():
                copy.wait_recv()

            def begin(piece, carry):
                lead[0, 0, piece, FACE:BOTH, width:whole_width] = inward(
                    start_left[piece], start_right[piece]
                )
                return carry

            lax.fori_loop(0, pieces, begin, 0)

        def one(piece, carry):
            step(piece)
            return carry

        def last(piece, carry):
            finish(sweep, piece)
            return carry

        lax.fori_loop(0, pieces, one, 0)
        lax.fori_loop(0, pieces, last, 0)

    first = (place >= flow_count // 2).astype(jnp.int32)
    on_end = jnp.logical_or(place == 0, place == flow_count - 1)

    def slot(at, carry):
        early = jnp.where(on_end, 2 + first, 1 - first)
        late_op = jnp.where(on_end, 1 - first, 2 + first)
        op = jnp.where(
            at == 0, first, jnp.where(at == 1, early, jnp.where(at == 2, late_op, 3 - first))
        )

        @pl.when(op == 0)
        def _():
            prepare(0)

        @pl.when(op == 1)
        def _():
            prepare(1)

        @pl.when(at == 0)
        def _():
            settle_facts()

        @pl.when(op == 2)
        def _():
            chain(0)

        @pl.when(op == 3)
        def _():
            chain(1)

        return carry

    lax.fori_loop(0, 4, slot, 0)

    for copy in fact_copies() + start_copies():
        copy.wait_send()

    @pl.when(below)
    def _():
        next_copy().wait_send()

    def settle(piece, carry):
        for copy in fix_copies(piece):
            copy.wait_send()
        for sweep in range(2):
            written(sweep, piece).wait()

            @pl.when(jnp.logical_not(is_last[sweep]))
            def _():
                for copy in wave_copies(sweep, piece):
                    copy.wait_send()

        return carry

    lax.fori_loop(0, pieces, settle, 0)


def per_device(
    source,
    cotangent,
    flux,
    pore_mask,
    upwind,
    side_link,
    local_inverse,
    flow_lift,
    side_lift,
    flow_trace,
    side_trace,
):
    levels, nodes, elems = source.shape
    tiles = elems // TILE
    pieces = tiles // GROUP
    width = GROUP * TILE
    extended = width + TILE
    whole = pl.BlockSpec(memory_space=pltpu.VMEM)
    away = pl.BlockSpec(memory_space=pltpu.HBM)
    dma = pltpu.SemaphoreType.DMA
    return pl.pallas_call(
        kernel,
        out_shape=(
            jax.ShapeDtypeStruct(source.shape, F32),
            jax.ShapeDtypeStruct(source.shape, F32),
        ),
        in_specs=[away, away] + [whole] * 9,
        out_specs=(away, away),
        scratch_shapes=[
            pltpu.VMEM((2, levels, nodes, elems), F32),
            pltpu.VMEM((2, levels, pieces, BOTH, extended), F32),
            pltpu.VMEM((levels, pieces, 1, extended), F32),
            pltpu.VMEM((levels, tiles, 2 * TILE, TILE), BF16),
            pltpu.VMEM((pieces, 2 * TILE, TILE), BF16),
            pltpu.VMEM((pieces, width, TILE), BF16),
            pltpu.VMEM((2, levels, pieces, 3 * BOTH, width), BF16),
            pltpu.VMEM((pieces, BOTH, width), F32),
            pltpu.VMEM((2, pieces, BOTH, extended), F32),
            pltpu.VMEM((2, pieces, BOTH, extended), F32),
            pltpu.VMEM((2, pieces, NEAR + FACE, TILE), F32),
            pltpu.VMEM((2, pieces, NEAR, TILE), F32),
            pltpu.VMEM((2, pieces, NEAR, TILE), F32),
            pltpu.VMEM((2, pieces, FACE, TILE), F32),
            pltpu.VMEM((2, pieces, FACE, TILE), F32),
            pltpu.VMEM((pieces, FACE, TILE), F32),
            pltpu.VMEM((pieces, FACE, TILE), F32),
            pltpu.VMEM((pieces, FACE, TILE), F32),
            pltpu.VMEM((pieces, 8, TILE), F32),
            pltpu.VMEM((pieces, 8, TILE), F32),
            pltpu.VMEM((pieces, 8, TILE), F32),
            pltpu.VMEM((pieces, 8, TILE), F32),
            pltpu.VMEM((pieces, FACE, TILE), F32),
            pltpu.VMEM((pieces, FACE, TILE), F32),
            pltpu.VMEM((pieces, FACE, TILE), F32),
            pltpu.VMEM((nodes, BOTH), F32),
            pltpu.VMEM((nodes + BOTH, 3 * nodes), F32),
            pltpu.VMEM((2, nodes + BOTH, 3 * nodes), BF16),
            pltpu.VMEM((2, BOTH, 3 * BOTH), BF16),
            pltpu.VMEM((2, nodes, 3 * BOTH), BF16),
            dma((2,)),
            dma((2, pieces)),
            dma((2, 2, pieces)),
            dma((4, 2, pieces)),
            dma((4, 2, pieces)),
            dma((4, pieces)),
            dma((4,)),
            dma((2,)),
            dma((4,)),
        ],
        compiler_params=pltpu.CompilerParams(
            collective_id=0, has_side_effects=True, vmem_limit_bytes=40 << 20
        ),
    )(
        source,
        cotangent,
        flux,
        pore_mask,
        upwind,
        side_link,
        local_inverse,
        flow_lift,
        side_lift,
        flow_trace,
        side_trace,
    )


def solution(mesh):
    placed = (
        P("flow", None, "cross"),
        P("flow", None, "cross"),
        P("flow", "cross"),
        P("flow", "cross"),
        P("flow", "cross"),
        P("flow", "cross"),
        P(),
        P(),
        P(),
        P(),
        P(),
    )
    return jax.shard_map(
        per_device,
        mesh=mesh,
        in_specs=placed,
        out_specs=(P("flow", None, "cross"), P("flow", None, "cross")),
        check_vma=False,
    )
```

```python
import jax
import jax.numpy as jnp
from jax import lax
from jax.experimental import pallas as pl
from jax.experimental.pallas import tpu as pltpu
from jax.sharding import PartitionSpec as P

FACE = 16
TILE = 128
HALO = 16
LEVELS_HERE = 2
GROUP = 4
HALF = TILE // 2
BOTH = 2 * FACE
NEAR = 3 * FACE
LIMIT = 60

HIGH = lax.Precision.HIGHEST
F32 = jnp.float32
BF16 = jnp.bfloat16
MESH = pl.DeviceIdType.MESH


def halves(value):
    high = value.astype(BF16)
    low = (value - high.astype(F32)).astype(BF16)
    return high, low


def stacked(value):
    high, low = halves(value)
    return jnp.concatenate([high, low, high], axis=0)


def product(left, right):
    return jnp.dot(left, right, preferred_element_type=F32)


def cross_product(left, right):
    return lax.dot_general(left, right, (((1,), (1,)), ((), ())), preferred_element_type=F32)


def widened(weight, wide, target):
    depth = weight.shape[1]
    high = weight.astype(BF16).astype(F32)
    wide[0 : weight.shape[0], 0:depth] = high
    wide[0 : weight.shape[0], depth : 2 * depth] = high
    wide[0 : weight.shape[0], 2 * depth : 3 * depth] = weight - high
    target[...] = wide[0 : weight.shape[0], 0 : 3 * depth].astype(BF16)


def kernel(
    source,
    cotangent,
    flux_away,
    pore_mask_away,
    upwind_away,
    side_link_away,
    local_inverse_away,
    flow_lift_rows,
    side_lift_rows,
    flow_trace,
    side_trace,
    concentration,
    sensitivity,
    field,
    lead,
    scale,
    pick,
    pick_beside,
    pick_next,
    kept,
    late,
    main_in,
    main_out,
    near_out,
    near_left,
    near_right,
    far_left,
    far_right,
    fix_out,
    fix_left,
    fix_right,
    fact_out,
    fact_left,
    fact_right,
    fact_next,
    start_out,
    start_left,
    start_right,
    flux,
    pore_mask,
    upwind,
    side_link,
    local_inverse,
    lift_rows,
    trace_rows,
    wide,
    local_weight,
    chain_weight,
    out_weight,
    small_sem,
    field_sem,
    done_sem,
    main_sem,
    near_sem,
    far_sem,
    fix_sem,
    fact_sem,
    next_sem,
    start_sem,
):
    flow_count = lax.axis_size("flow")
    cross_count = lax.axis_size("cross")
    place = lax.axis_index("flow")
    block = lax.axis_index("cross")
    pieces = main_in.shape[1]
    whole_width = main_in.shape[3]
    width = whole_width - TILE
    nodes = field.shape[2]
    inputs = (source, cotangent)
    results = (concentration, sensitivity)
    is_first = (place == 0, place == flow_count - 1)
    is_last = (place == flow_count - 1, place == 0)
    downstream = (place + 1, place - 1)
    below, above = place > 0, place < flow_count - 1

    def inside(steps):
        return (block + steps >= 0) & (block + steps < cross_count)

    def loaded(sweep):
        return pltpu.make_async_copy(inputs[sweep], field.at[sweep], field_sem.at[sweep])

    small = (
        (side_link_away, side_link),
        (upwind_away, upwind),
        (flux_away, flux),
        (pore_mask_away, pore_mask),
        (local_inverse_away, local_inverse),
        (flow_trace, trace_rows.at[pl.ds(0, FACE)]),
        (side_trace, trace_rows.at[pl.ds(FACE, FACE)]),
        (flow_lift_rows, lift_rows.at[pl.ds(0, FACE)]),
        (side_lift_rows, lift_rows.at[pl.ds(FACE, FACE)]),
    )
    fetches = [
        pltpu.make_async_copy(src, dst, small_sem.at[n]) for n, (src, dst) in enumerate(small)
    ]
    for fetch in fetches:
        fetch.start()

    @pl.when(above)
    def _():
        loaded(0).start()
        loaded(1).start()

    @pl.when(jnp.logical_not(above))
    def _():
        loaded(1).start()
        loaded(0).start()

    barrier = pltpu.get_barrier_semaphore()

    def greet(flow_at, steps):
        @pl.when(inside(steps))
        def _():
            pl.semaphore_signal(
                barrier, inc=1, device_id=(flow_at, block + steps), device_id_type=MESH
            )

    greet(place, -1)
    greet(place, 1)

    @pl.when(below)
    def _():
        for steps in range(-2, 3):
            greet(place - 1, steps)

    @pl.when(above)
    def _():
        for steps in range(-2, 3):
            greet(place + 1, steps)

    in_line = [inside(steps).astype(jnp.int32) for steps in range(-2, 3)]
    met = (below.astype(jnp.int32) + above.astype(jnp.int32)) * sum(in_line)
    met = met + in_line[1] + in_line[3]

    for fetch in fetches:
        fetch.wait()

    inverse = local_inverse[...]
    lifts = lift_rows[...].T
    trace = trace_rows[...]
    traced_inverse = jnp.dot(trace, inverse, precision=HIGH, preferred_element_type=F32)
    traced_lift = jnp.dot(trace, lifts, precision=HIGH, preferred_element_type=F32)
    widened(jnp.concatenate([inverse, traced_inverse], axis=0), wide, local_weight.at[0])
    widened(jnp.concatenate([inverse.T, lift_rows[...]], axis=0), wide, local_weight.at[1])
    widened(traced_lift, wide, chain_weight.at[0])
    widened(traced_lift.T, wide, chain_weight.at[1])
    widened(lifts, wide, out_weight.at[0])
    widened(traced_inverse.T, wide, out_weight.at[1])

    def lanes(rows):
        return lax.broadcasted_iota(jnp.int32, (rows, TILE), 1)

    def packed(value):
        lane = lanes(value.shape[0])
        edge = jnp.zeros(lane.shape, F32)
        for at in range(GROUP):
            tile = value[:, at * TILE : (at + 1) * TILE]
            start = at * HALO
            tail = pltpu.roll(tile, (start + HALO) % TILE, 1)
            head = pltpu.roll(tile, (start + HALF) % TILE, 1)
            edge = jnp.where((lane >= start) & (lane < start + HALO), tail, edge)
            edge = jnp.where((lane >= start + HALF) & (lane < start + HALF + HALO), head, edge)
        return edge

    def unpacked(edge, at):
        lane = lanes(edge.shape[0])
        start = at * HALO
        head = pltpu.roll(edge, (TILE - HALF - start) % TILE, 1)
        tail = pltpu.roll(edge, (TILE - HALO - start) % TILE, 1)
        return jnp.where(lane < HALO, head, jnp.where(lane >= TILE - HALO, tail, 0.0))

    def is_open(reach):
        return (
            (block >= reach).astype(jnp.int32),
            (block < cross_count - reach).astype(jnp.int32),
        )

    def inward(from_left, from_right, reach=1):
        lane = lanes(from_left.shape[0])
        opened = jnp.where(lane < HALF, *is_open(reach))
        return jnp.where(opened > 0, jnp.where(lane < HALF, from_left, from_right), 0.0)

    def homeward(from_left, from_right, reach=1):
        lane = lanes(from_left.shape[0])
        opened = jnp.where(lane < HALF, *is_open(reach)[::-1])
        return jnp.where(opened > 0, jnp.where(lane < HALF, from_right, from_left), 0.0)

    def columns_of(piece):
        return pl.ds(pl.multiple_of(piece * width, width), width)

    def live(level, piece):
        return pore_mask[level : level + 1, columns_of(piece)].astype(F32)

    def codes(level, piece):
        cols = columns_of(piece)
        inflow = upwind[level : level + 1, cols]
        return jnp.where(inflow != 0, side_link[level : level + 1, cols], -1)

    def gather_facts(piece, carry):
        for level in range(LEVELS_HERE):
            cols = columns_of(piece)
            scale[level, piece, :, 0:width] = live(level, piece) * flux[level : level + 1, cols]
        rows = jnp.concatenate(
            [
                scale[0, piece, :, 0:width],
                codes(0, piece).astype(F32),
                jnp.zeros((6, width), F32),
            ],
            axis=0,
        )
        fact_out[piece] = packed(rows)
        return carry

    lax.fori_loop(0, pieces, gather_facts, 0)

    def send(src, dst, send_sem, recv_sem, flow_at, steps):
        copy = pltpu.make_async_remote_copy(
            src_ref=src,
            dst_ref=dst,
            send_sem=send_sem,
            recv_sem=recv_sem,
            device_id=(flow_at, block + steps),
            device_id_type=MESH,
        )
        return copy, steps

    def pair(src, at_left, at_right, sem, flow_at, reach=1):
        return (
            send(src, at_left, sem(0), sem(1), flow_at, reach),
            send(src, at_right, sem(2), sem(3), flow_at, -reach),
        )

    def each(copies, act, sign):
        for copy, steps in copies:
            if steps == 0:
                act(copy)
            else:
                pl.when(inside(sign * steps))(lambda copy=copy: act(copy))

    def start_all(copies):
        each(copies, lambda copy: copy.start(), 1)

    def wait_sent(copies):
        each(copies, lambda copy: copy.wait_send(), 1)

    def wait_received(copies):
        each(copies, lambda copy: copy.wait_recv(), -1)

    def fact_copies():
        return pair(fact_out, fact_left, fact_right, lambda n: fact_sem.at[n], place)

    def next_copies():
        return (send(fact_out, fact_next, next_sem.at[0], next_sem.at[1], place - 1, 0),)

    def start_copies():
        return pair(start_out, start_left, start_right, lambda n: start_sem.at[n], place)

    def fix_copies(piece):
        return pair(
            fix_out.at[piece],
            fix_left.at[piece],
            fix_right.at[piece],
            lambda n: fix_sem.at[n, piece],
            place,
        )

    def wave_copies(sweep, piece):
        flow_at = downstream[sweep]
        main = send(
            main_out.at[sweep, piece],
            main_in.at[sweep, piece],
            main_sem.at[0, sweep, piece],
            main_sem.at[1, sweep, piece],
            flow_at,
            0,
        )
        near = pair(
            near_out.at[sweep, piece, pl.ds(0, NEAR)],
            near_left.at[sweep, piece],
            near_right.at[sweep, piece],
            lambda n: near_sem.at[n, sweep, piece],
            flow_at,
        )
        far = pair(
            near_out.at[sweep, piece, pl.ds(NEAR, FACE)],
            far_left.at[sweep, piece],
            far_right.at[sweep, piece],
            lambda n: far_sem.at[n, sweep, piece],
            flow_at,
            2,
        )
        return near + far + (main,)

    pl.semaphore_wait(barrier, met)

    start_all(fact_copies())

    @pl.when(below)
    def _():
        start_all(next_copies())

    def one_hot(row, depth):
        rows = lax.broadcasted_iota(jnp.int32, (depth, TILE), 0)
        return jnp.where(rows == row, 1.0, 0.0).astype(BF16)

    def build_pick(piece, carry):
        for level in range(LEVELS_HERE):
            code = codes(level, piece)
            for at in range(GROUP):
                link = code[:, at * TILE : (at + 1) * TILE]
                row = jnp.where(
                    link < HALO,
                    link + (TILE + at * HALO),
                    jnp.where(
                        link < HALO + TILE, link - HALO, link + (HALF + at * HALO - HALO)
                    ),
                )
                row = jnp.where(link >= 0, row, -1)
                pick[level, piece * GROUP + at] = one_hot(row, 2 * TILE)
        return carry

    lax.fori_loop(0, pieces, build_pick, 0)

    def settle_facts():
        wait_received(fact_copies())

        @pl.when(above)
        def _():
            wait_received(next_copies())

        @pl.when(jnp.logical_not(above))
        def _():
            fact_next[...] = jnp.zeros(fact_next.shape, F32)

        lane = lanes(1)
        start = lax.rem(lane, HALF) // HALO * HALO
        on_left = lane < HALF

        def one(piece, carry):
            facts = inward(fact_left[piece], fact_right[piece])
            scale[0, piece, :, width:whole_width] = facts[0:1]
            link = facts[1:2].astype(jnp.int32)
            low = (link >= 0) & (link < HALO)
            high = link >= HALO + TILE
            after = link - (HALO + TILE)
            left_row = jnp.where(
                high, HALF + start + after, jnp.where(low, TILE + start + link, -1)
            )
            right_row = jnp.where(
                low, start + link, jnp.where(high, TILE + HALF + start + after, -1)
            )
            pick_beside[piece] = one_hot(jnp.where(on_left, left_row, right_row), 2 * TILE)
            link = fact_next[piece][1:2].astype(jnp.int32)
            inside = (link >= HALO) & (link < HALO + TILE)
            row = jnp.where(inside, start * (TILE // HALO) + link - HALO, -1)
            pick_next[piece] = one_hot(row, width)
            return carry

        lax.fori_loop(0, pieces, one, 0)

    def prepare(sweep):
        loaded(sweep).wait()

        def one(level, piece):
            cols = columns_of(piece)
            value = product(local_weight[sweep], stacked(field[sweep, level, :, cols]))
            mask = live(level, piece)
            field[sweep, level, :, cols] = mask * value[:nodes]
            added = (mask if sweep == 0 else scale[level, piece, :, 0:width]) * value[nodes:]
            lead[sweep, level, piece, :, 0:width] = added
            if level == 0:
                lead[sweep, 0, piece, :, width:whole_width] = jnp.zeros((BOTH, TILE), F32)
                if sweep == 0:
                    start_out[piece] = packed(added[FACE:])

        def first_level(piece, carry):
            one(0, piece)
            return carry

        def second_level(piece, carry):
            one(1, piece)
            return carry

        lax.fori_loop(0, pieces, first_level, 0)
        if sweep == 0:
            start_all(start_copies())
        lax.fori_loop(0, pieces, second_level, 0)

    def arrive(sweep, piece):
        @pl.when(is_first[sweep])
        def _():
            main_in[sweep, piece] = jnp.zeros((BOTH, whole_width), F32)
            near_left[sweep, piece] = jnp.zeros((NEAR, TILE), F32)
            near_right[sweep, piece] = jnp.zeros((NEAR, TILE), F32)
            far_left[sweep, piece] = jnp.zeros((FACE, TILE), F32)
            far_right[sweep, piece] = jnp.zeros((FACE, TILE), F32)

        @pl.when(jnp.logical_not(is_first[sweep]))
        def _():
            wait_received(wave_copies(sweep, piece))

    def leave(sweep, piece):
        start_all(wave_copies(sweep, piece))

    def picked(near, beyond, one_hots):
        near_high, near_low = near
        beyond_high, beyond_low = beyond
        extended = jnp.concatenate(
            [
                jnp.concatenate([near_high, beyond_high], axis=1),
                jnp.concatenate([near_low, beyond_low], axis=1),
            ],
            axis=0,
        )
        value = product(extended, one_hots)
        return value[:FACE] + value[FACE:]

    def spread(value, one_hots):
        value = cross_product(jnp.concatenate(halves(value), axis=0), one_hots)
        return value[:FACE] + value[FACE:]

    def cut(value, at):
        return value[:, at * TILE : (at + 1) * TILE]

    def gathered(sides, halo, level, piece):
        halo = halves(halo)
        high, low = halves(sides)
        return [
            picked((cut(high, at), cut(low, at)), halo, pick[level, piece * GROUP + at])
            for at in range(GROUP)
        ]

    def scattered(sides, level, piece):
        own = []
        edge = jnp.zeros((FACE, TILE), F32)
        for at in range(GROUP):
            value = spread(cut(sides, at), pick[level, piece * GROUP + at])
            own.append(value[:, :TILE])
            edge = edge + value[:, TILE:]
        return own, edge

    def forward(piece):
        arrive(0, piece)
        main = main_in[0, piece]
        near = inward(near_left[0, piece], near_right[0, piece])
        outer = inward(far_left[0, piece], far_right[0, piece], 2)
        sides = gathered(main[FACE:, :width], near[BOTH:], 0, piece)
        sides.append(
            near[FACE:BOTH]
            + picked(halves(main[FACE:, width:]), halves(outer), pick_beside[piece])
        )
        inbound = jnp.concatenate(
            [
                jnp.concatenate([main[:FACE, :width], near[:FACE]], axis=1),
                jnp.concatenate(sides, axis=1),
            ],
            axis=0,
        )
        operand = stacked(inbound)
        kept[0, 0, piece] = operand[:, :width]
        value = lead[0, 0, piece] + scale[0, piece] * product(chain_weight[0], operand)
        sides = gathered(value[FACE:, :width], value[FACE:, width:], 1, piece)
        operand = stacked(
            jnp.concatenate([value[:FACE, :width], jnp.concatenate(sides, axis=1)], axis=0)
        )
        kept[0, 1, piece] = operand

        @pl.when(jnp.logical_not(is_last[0]))
        def _():
            value = lead[0, 1, piece, :, 0:width] + scale[1, piece, :, 0:width] * product(
                chain_weight[0], operand
            )
            edges = packed(value)
            ahead = product(jnp.concatenate(halves(value[FACE:]), axis=0), pick_next[piece])
            main_out[0, piece, :, 0:width] = value
            main_out[0, piece, :, width:whole_width] = edges
            near_out[0, piece, 0:FACE] = edges[:FACE]
            near_out[0, piece, FACE:BOTH] = ahead[:FACE] + ahead[FACE:]
            near_out[0, piece, BOTH:NEAR] = edges[FACE:]
            near_out[0, piece, NEAR : NEAR + FACE] = edges[FACE:]
            leave(0, piece)

    def adjoint(piece):
        arrive(1, piece)
        main = main_in[1, piece]
        near = homeward(near_left[1, piece], near_right[1, piece])
        outer = homeward(far_left[1, piece], far_right[1, piece], 2)
        edges = jnp.concatenate(
            [near[:FACE], main[FACE:, width:] + near[BOTH:] + outer], axis=0
        )
        behind = spread(near[FACE:BOTH], pick_next[piece])
        none = jnp.zeros((FACE, TILE), F32)
        inbound = jnp.concatenate(
            [
                cut(main, at)
                + unpacked(edges, at)
                + jnp.concatenate([none, cut(behind, at)], axis=0)
                for at in range(GROUP)
            ],
            axis=1,
        )
        operand = stacked(inbound)
        kept[1, 1, piece] = operand
        value = lead[1, 1, piece, :, 0:width] + scale[1, piece, :, 0:width] * product(
            chain_weight[1], operand
        )
        own, edge = scattered(value[FACE:], 1, piece)
        fix_out[piece] = edge
        start_all(fix_copies(piece))
        inbound = jnp.concatenate(
            [
                jnp.concatenate([value[:FACE], none], axis=1),
                jnp.concatenate(own + [edge], axis=1),
            ],
            axis=0,
        )
        late[piece] = inbound[:, :width]

        @pl.when(jnp.logical_not(is_last[1]))
        def _():
            value = lead[1, 0, piece] + scale[0, piece] * product(
                chain_weight[1], stacked(inbound)
            )
            own, edge = scattered(value[FACE:, :width], 0, piece)
            around = spread(value[FACE:, width:], pick_beside[piece])
            own.append(around[:, :TILE])
            main_out[1, piece, 0:FACE] = jnp.concatenate([value[:FACE, :width], none], axis=1)
            main_out[1, piece, FACE:BOTH] = jnp.concatenate(own, axis=1)
            near_out[1, piece, 0:BOTH] = value[:, width:]
            near_out[1, piece, BOTH:NEAR] = edge
            near_out[1, piece, NEAR : NEAR + FACE] = around[:, TILE:]
            leave(1, piece)

    def written(sweep, piece):
        cols = columns_of(piece)
        return pltpu.make_async_copy(
            field.at[sweep, :, :, cols], results[sweep].at[:, :, cols], done_sem.at[sweep, piece]
        )

    def finish(sweep, piece):
        cols = columns_of(piece)
        for level in range(LEVELS_HERE):
            if sweep == 1 and level == 0:
                wait_received(fix_copies(piece))
                edges = homeward(fix_left[piece], fix_right[piece])
                sides = [
                    cut(late[piece, FACE:BOTH], at) + unpacked(edges, at) for at in range(GROUP)
                ]
                operand = stacked(
                    jnp.concatenate(
                        [late[piece, 0:FACE], jnp.concatenate(sides, axis=1)], axis=0
                    )
                )
            else:
                operand = kept[sweep, level, piece]
            factor = scale[level, piece, :, 0:width] if sweep == 0 else live(level, piece)
            field[sweep, level, :, cols] += factor * product(out_weight[sweep], operand)
        written(sweep, piece).start()

    def chain(sweep):
        step = forward if sweep == 0 else adjoint
        if sweep == 0:
            wait_received(start_copies())

            def begin(piece, carry):
                lead[0, 0, piece, FACE:BOTH, width:whole_width] = inward(
                    start_left[piece], start_right[piece]
                )
                return carry

            lax.fori_loop(0, pieces, begin, 0)

        def one(piece, carry):
            step(piece)
            return carry

        def last(piece, carry):
            finish(sweep, piece)
            return carry

        lax.fori_loop(0, pieces, one, 0)
        lax.fori_loop(0, pieces, last, 0)

    first = (place >= flow_count // 2).astype(jnp.int32)
    on_end = jnp.logical_or(place == 0, place == flow_count - 1)

    def slot(at, carry):
        early = jnp.where(on_end, 2 + first, 1 - first)
        late_op = jnp.where(on_end, 1 - first, 2 + first)
        op = jnp.where(
            at == 0, first, jnp.where(at == 1, early, jnp.where(at == 2, late_op, 3 - first))
        )

        @pl.when(op == 0)
        def _():
            prepare(0)

        @pl.when(op == 1)
        def _():
            prepare(1)

        @pl.when(at == 0)
        def _():
            settle_facts()

        @pl.when(op == 2)
        def _():
            chain(0)

        @pl.when(op == 3)
        def _():
            chain(1)

        return carry

    lax.fori_loop(0, 4, slot, 0)

    wait_sent(fact_copies() + start_copies())

    @pl.when(below)
    def _():
        wait_sent(next_copies())

    def settle(piece, carry):
        wait_sent(fix_copies(piece))
        for sweep in range(2):
            written(sweep, piece).wait()

            @pl.when(jnp.logical_not(is_last[sweep]))
            def _():
                wait_sent(wave_copies(sweep, piece))

        return carry

    lax.fori_loop(0, pieces, settle, 0)


def per_device(
    source,
    cotangent,
    flux,
    pore_mask,
    upwind,
    side_link,
    local_inverse,
    flow_lift,
    side_lift,
    flow_trace,
    side_trace,
):
    levels, nodes, elems = source.shape
    tiles = elems // TILE
    pieces = tiles // GROUP
    width = GROUP * TILE
    extended = width + TILE
    away = pl.BlockSpec(memory_space=pltpu.HBM)
    dma = pltpu.SemaphoreType.DMA
    return pl.pallas_call(
        kernel,
        out_shape=(
            jax.ShapeDtypeStruct(source.shape, F32),
            jax.ShapeDtypeStruct(source.shape, F32),
        ),
        in_specs=[away] * 11,
        out_specs=(away, away),
        scratch_shapes=[
            pltpu.VMEM((2, levels, nodes, elems), F32),
            pltpu.VMEM((2, levels, pieces, BOTH, extended), F32),
            pltpu.VMEM((levels, pieces, 1, extended), F32),
            pltpu.VMEM((levels, tiles, 2 * TILE, TILE), BF16),
            pltpu.VMEM((pieces, 2 * TILE, TILE), BF16),
            pltpu.VMEM((pieces, width, TILE), BF16),
            pltpu.VMEM((2, levels, pieces, 3 * BOTH, width), BF16),
            pltpu.VMEM((pieces, BOTH, width), F32),
            pltpu.VMEM((2, pieces, BOTH, extended), F32),
            pltpu.VMEM((2, pieces, BOTH, extended), F32),
            pltpu.VMEM((2, pieces, NEAR + FACE, TILE), F32),
            pltpu.VMEM((2, pieces, NEAR, TILE), F32),
            pltpu.VMEM((2, pieces, NEAR, TILE), F32),
            pltpu.VMEM((2, pieces, FACE, TILE), F32),
            pltpu.VMEM((2, pieces, FACE, TILE), F32),
            pltpu.VMEM((pieces, FACE, TILE), F32),
            pltpu.VMEM((pieces, FACE, TILE), F32),
            pltpu.VMEM((pieces, FACE, TILE), F32),
            pltpu.VMEM((pieces, 8, TILE), F32),
            pltpu.VMEM((pieces, 8, TILE), F32),
            pltpu.VMEM((pieces, 8, TILE), F32),
            pltpu.VMEM((pieces, 8, TILE), F32),
            pltpu.VMEM((pieces, FACE, TILE), F32),
            pltpu.VMEM((pieces, FACE, TILE), F32),
            pltpu.VMEM((pieces, FACE, TILE), F32),
            pltpu.VMEM((levels, elems), F32),
            pltpu.VMEM((levels, elems), jnp.int32),
            pltpu.VMEM((levels, elems), jnp.int32),
            pltpu.VMEM((levels, elems), jnp.int32),
            pltpu.VMEM((nodes, nodes), F32),
            pltpu.VMEM((BOTH, nodes), F32),
            pltpu.VMEM((BOTH, nodes), F32),
            pltpu.VMEM((nodes + BOTH, 3 * nodes), F32),
            pltpu.VMEM((2, nodes + BOTH, 3 * nodes), BF16),
            pltpu.VMEM((2, BOTH, 3 * BOTH), BF16),
            pltpu.VMEM((2, nodes, 3 * BOTH), BF16),
            dma((9,)),
            dma((2,)),
            dma((2, pieces)),
            dma((2, 2, pieces)),
            dma((4, 2, pieces)),
            dma((4, 2, pieces)),
            dma((4, pieces)),
            dma((4,)),
            dma((2,)),
            dma((4,)),
        ],
        compiler_params=pltpu.CompilerParams(
            collective_id=0, has_side_effects=True, vmem_limit_bytes=LIMIT << 20
        ),
    )(
        source,
        cotangent,
        flux,
        pore_mask,
        upwind,
        side_link,
        local_inverse,
        flow_lift.T,
        side_lift.T,
        flow_trace,
        side_trace,
    )


def solution(mesh):
    placed = (
        P("flow", None, "cross"),
        P("flow", None, "cross"),
        P("flow", "cross"),
        P("flow", "cross"),
        P("flow", "cross"),
        P("flow", "cross"),
        P(),
        P(),
        P(),
        P(),
        P(),
    )
    return jax.shard_map(
        per_device,
        mesh=mesh,
        in_specs=placed,
        out_specs=(P("flow", None, "cross"), P("flow", None, "cross")),
        check_vma=False,
    )
```

```python
import jax
import jax.numpy as jnp
from jax import lax
from jax.experimental import pallas as pl
from jax.experimental.pallas import tpu as pltpu
from jax.sharding import PartitionSpec as P

FACE = 16
TILE = 128
HALO = 16
LEVELS_HERE = 2
GROUP = 4
HALF = TILE // 2
BOTH = 2 * FACE
NEAR = 2 * FACE
LIMIT = 48

HIGH = lax.Precision.HIGHEST
F32 = jnp.float32
BF16 = jnp.bfloat16
MESH = pl.DeviceIdType.MESH


def halves(value):
    high = value.astype(BF16)
    low = (value - high.astype(F32)).astype(BF16)
    return high, low


def stacked(value):
    high, low = halves(value)
    return jnp.concatenate([high, low, high], axis=0)


def product(left, right):
    return jnp.dot(left, right, preferred_element_type=F32)


def cross_product(left, right):
    return lax.dot_general(left, right, (((1,), (1,)), ((), ())), preferred_element_type=F32)


def widened(weight, wide, target):
    depth = weight.shape[1]
    high = weight.astype(BF16).astype(F32)
    wide[0 : weight.shape[0], 0:depth] = high
    wide[0 : weight.shape[0], depth : 2 * depth] = high
    wide[0 : weight.shape[0], 2 * depth : 3 * depth] = weight - high
    target[...] = wide[0 : weight.shape[0], 0 : 3 * depth].astype(BF16)


def kernel(
    source,
    cotangent,
    flux_away,
    pore_mask_away,
    upwind_away,
    side_link_away,
    local_inverse_away,
    flow_lift_rows,
    side_lift_rows,
    flow_trace,
    side_trace,
    concentration,
    sensitivity,
    lead,
    scale,
    pick,
    pick_beside,
    pick_next,
    kept,
    late,
    main_in,
    main_out,
    near_out,
    near_left,
    near_right,
    far_left,
    far_right,
    fix_out,
    fix_left,
    fix_right,
    fact_out,
    fact_left,
    fact_right,
    fact_next,
    start_out,
    start_left,
    start_right,
    flux,
    pore_mask,
    upwind,
    side_link,
    local_inverse,
    lift_rows,
    trace_rows,
    wide,
    local_weight,
    chain_weight,
    out_weight,
    small_sem,
    field_sem,
    main_sem,
    near_sem,
    far_sem,
    fix_sem,
    fact_sem,
    next_sem,
    start_sem,
):
    flow_count = lax.axis_size("flow")
    cross_count = lax.axis_size("cross")
    place = lax.axis_index("flow")
    block = lax.axis_index("cross")
    pieces = main_in.shape[1]
    width = main_in.shape[3]
    whole_width = width + TILE
    nodes = concentration.shape[1]
    inputs = (source, cotangent)
    results = (concentration, sensitivity)
    is_first = (place == 0, place == flow_count - 1)
    is_last = (place == flow_count - 1, place == 0)
    downstream = (place + 1, place - 1)
    below, above = place > 0, place < flow_count - 1

    def inside(steps):
        return (block + steps >= 0) & (block + steps < cross_count)

    def loaded(sweep):
        return pltpu.make_async_copy(inputs[sweep], results[sweep], field_sem.at[sweep])

    small = (
        (side_link_away, side_link),
        (upwind_away, upwind),
        (flux_away, flux),
        (pore_mask_away, pore_mask),
        (local_inverse_away, local_inverse),
        (flow_trace, trace_rows.at[pl.ds(0, FACE)]),
        (side_trace, trace_rows.at[pl.ds(FACE, FACE)]),
        (flow_lift_rows, lift_rows.at[pl.ds(0, FACE)]),
        (side_lift_rows, lift_rows.at[pl.ds(FACE, FACE)]),
    )
    fetches = [
        pltpu.make_async_copy(src, dst, small_sem.at[n]) for n, (src, dst) in enumerate(small)
    ]
    for fetch in fetches:
        fetch.start()

    @pl.when(above)
    def _():
        loaded(0).start()
        loaded(1).start()

    @pl.when(jnp.logical_not(above))
    def _():
        loaded(1).start()
        loaded(0).start()

    barrier = pltpu.get_barrier_semaphore()

    def greet(flow_at, steps):
        @pl.when(inside(steps))
        def _():
            pl.semaphore_signal(
                barrier, inc=1, device_id=(flow_at, block + steps), device_id_type=MESH
            )

    greet(place, -1)
    greet(place, 1)

    @pl.when(below)
    def _():
        for steps in range(-2, 3):
            greet(place - 1, steps)

    @pl.when(above)
    def _():
        for steps in range(-2, 3):
            greet(place + 1, steps)

    in_line = [inside(steps).astype(jnp.int32) for steps in range(-2, 3)]
    met = (below.astype(jnp.int32) + above.astype(jnp.int32)) * sum(in_line)
    met = met + in_line[1] + in_line[3]

    for fetch in fetches:
        fetch.wait()

    inverse = local_inverse[...]
    lifts = lift_rows[...].T
    trace = trace_rows[...]
    traced_inverse = jnp.dot(trace, inverse, precision=HIGH, preferred_element_type=F32)
    traced_lift = jnp.dot(trace, lifts, precision=HIGH, preferred_element_type=F32)
    widened(jnp.concatenate([inverse, traced_inverse], axis=0), wide, local_weight.at[0])
    widened(jnp.concatenate([inverse.T, lift_rows[...]], axis=0), wide, local_weight.at[1])
    widened(traced_lift, wide, chain_weight.at[0])
    widened(traced_lift.T, wide, chain_weight.at[1])
    widened(lifts, wide, out_weight.at[0])
    widened(traced_inverse.T, wide, out_weight.at[1])

    def lanes(rows):
        return lax.broadcasted_iota(jnp.int32, (rows, TILE), 1)

    def packed(value):
        lane = lanes(value.shape[0])
        edge = jnp.zeros(lane.shape, F32)
        for at in range(GROUP):
            tile = value[:, at * TILE : (at + 1) * TILE]
            start = at * HALO
            tail = pltpu.roll(tile, (start + HALO) % TILE, 1)
            head = pltpu.roll(tile, (start + HALF) % TILE, 1)
            edge = jnp.where((lane >= start) & (lane < start + HALO), tail, edge)
            edge = jnp.where((lane >= start + HALF) & (lane < start + HALF + HALO), head, edge)
        return edge

    def unpacked(edge, at):
        lane = lanes(edge.shape[0])
        start = at * HALO
        head = pltpu.roll(edge, (TILE - HALF - start) % TILE, 1)
        tail = pltpu.roll(edge, (TILE - HALO - start) % TILE, 1)
        return jnp.where(lane < HALO, head, jnp.where(lane >= TILE - HALO, tail, 0.0))

    def is_open(reach):
        return (
            (block >= reach).astype(jnp.int32),
            (block < cross_count - reach).astype(jnp.int32),
        )

    def inward(from_left, from_right, reach=1):
        lane = lanes(from_left.shape[0])
        opened = jnp.where(lane < HALF, *is_open(reach))
        return jnp.where(opened > 0, jnp.where(lane < HALF, from_left, from_right), 0.0)

    def homeward(from_left, from_right, reach=1):
        lane = lanes(from_left.shape[0])
        opened = jnp.where(lane < HALF, *is_open(reach)[::-1])
        return jnp.where(opened > 0, jnp.where(lane < HALF, from_right, from_left), 0.0)

    def swapped(value):
        return pltpu.roll(value, HALF, 1)

    def folded(first, second, third):
        lane = lanes(FACE)
        low = jnp.where(lane < HALF, first, swapped(second))
        high = jnp.where(lane < HALF, swapped(first), second)
        return jnp.concatenate([low, third, high], axis=0)

    def unfolded(lows, highs):
        low = jnp.concatenate([lows[:FACE], swapped(lows[:FACE]), lows[FACE:]], axis=0)
        high = jnp.concatenate([swapped(highs[FACE:]), highs[FACE:], highs[:FACE]], axis=0)
        return low, high

    def columns_of(piece):
        return pl.ds(pl.multiple_of(piece * width, width), width)

    def live(level, piece):
        return pore_mask[level : level + 1, columns_of(piece)].astype(F32)

    def codes(level, piece):
        cols = columns_of(piece)
        inflow = upwind[level : level + 1, cols]
        return jnp.where(inflow != 0, side_link[level : level + 1, cols], -1)

    def gather_facts(piece, carry):
        for level in range(LEVELS_HERE):
            cols = columns_of(piece)
            scale[level, piece, :, 0:width] = live(level, piece) * flux[level : level + 1, cols]
        rows = jnp.concatenate(
            [
                scale[0, piece, :, 0:width],
                codes(0, piece).astype(F32),
                jnp.zeros((6, width), F32),
            ],
            axis=0,
        )
        fact_out[piece] = packed(rows)
        return carry

    lax.fori_loop(0, pieces, gather_facts, 0)

    def send(src, dst, send_sem, recv_sem, flow_at, steps):
        copy = pltpu.make_async_remote_copy(
            src_ref=src,
            dst_ref=dst,
            send_sem=send_sem,
            recv_sem=recv_sem,
            device_id=(flow_at, block + steps),
            device_id_type=MESH,
        )
        return copy, steps

    def pair(src, at_left, at_right, sem, flow_at, reach=1):
        return (
            send(src, at_left, sem(0), sem(1), flow_at, reach),
            send(src, at_right, sem(2), sem(3), flow_at, -reach),
        )

    def each(copies, act, sign):
        for copy, steps in copies:
            if steps == 0:
                act(copy)
            else:
                pl.when(inside(sign * steps))(lambda copy=copy: act(copy))

    def start_all(copies):
        each(copies, lambda copy: copy.start(), 1)

    def wait_sent(copies):
        each(copies, lambda copy: copy.wait_send(), 1)

    def wait_received(copies):
        each(copies, lambda copy: copy.wait_recv(), -1)

    def fact_copies():
        return pair(fact_out, fact_left, fact_right, lambda n: fact_sem.at[n], place)

    def next_copies():
        return (send(fact_out, fact_next, next_sem.at[0], next_sem.at[1], place - 1, 0),)

    def start_copies():
        return pair(start_out, start_left, start_right, lambda n: start_sem.at[n], place)

    def fix_copies(piece):
        return pair(
            fix_out.at[piece],
            fix_left.at[piece],
            fix_right.at[piece],
            lambda n: fix_sem.at[n, piece],
            place,
        )

    def wave_copies(sweep, piece):
        flow_at = downstream[sweep]
        main = send(
            main_out.at[sweep, piece],
            main_in.at[sweep, piece],
            main_sem.at[0, sweep, piece],
            main_sem.at[1, sweep, piece],
            flow_at,
            0,
        )
        low = near_out.at[sweep, piece, pl.ds(0, NEAR)]
        high = near_out.at[sweep, piece, pl.ds(FACE, NEAR)]
        ahead, back = (low, high) if sweep == 0 else (high, low)
        near = (
            send(
                ahead,
                near_left.at[sweep, piece],
                near_sem.at[0, sweep, piece],
                near_sem.at[1, sweep, piece],
                flow_at,
                1,
            ),
            send(
                back,
                near_right.at[sweep, piece],
                near_sem.at[2, sweep, piece],
                near_sem.at[3, sweep, piece],
                flow_at,
                -1,
            ),
        )
        far = pair(
            near_out.at[sweep, piece, pl.ds(FACE if sweep == 0 else 3 * FACE, FACE)],
            far_left.at[sweep, piece],
            far_right.at[sweep, piece],
            lambda n: far_sem.at[n, sweep, piece],
            flow_at,
            2,
        )
        return near + far + (main,)

    pl.semaphore_wait(barrier, met)

    start_all(fact_copies())

    @pl.when(below)
    def _():
        start_all(next_copies())

    def one_hot(row, depth):
        rows = lax.broadcasted_iota(jnp.int32, (depth, TILE), 0)
        return jnp.where(rows == row, 1.0, 0.0).astype(BF16)

    def build_pick(piece, carry):
        for level in range(LEVELS_HERE):
            code = codes(level, piece)
            for at in range(GROUP):
                link = code[:, at * TILE : (at + 1) * TILE]
                row = jnp.where(
                    link < HALO,
                    link + (TILE + at * HALO),
                    jnp.where(
                        link < HALO + TILE, link - HALO, link + (HALF + at * HALO - HALO)
                    ),
                )
                row = jnp.where(link >= 0, row, -1)
                pick[level, piece * GROUP + at] = one_hot(row, 2 * TILE)
        return carry

    lax.fori_loop(0, pieces, build_pick, 0)

    def settle_facts():
        wait_received(fact_copies())

        @pl.when(above)
        def _():
            wait_received(next_copies())

        @pl.when(jnp.logical_not(above))
        def _():
            fact_next[...] = jnp.zeros(fact_next.shape, F32)

        lane = lanes(1)
        start = lax.rem(lane, HALF) // HALO * HALO
        on_left = lane < HALF

        def one(piece, carry):
            facts = inward(fact_left[piece], fact_right[piece])
            scale[0, piece, :, width:whole_width] = facts[0:1]
            link = facts[1:2].astype(jnp.int32)
            low = (link >= 0) & (link < HALO)
            high = link >= HALO + TILE
            after = link - (HALO + TILE)
            left_row = jnp.where(
                high, HALF + start + after, jnp.where(low, TILE + start + link, -1)
            )
            right_row = jnp.where(
                low, start + link, jnp.where(high, TILE + HALF + start + after, -1)
            )
            pick_beside[piece] = one_hot(jnp.where(on_left, left_row, right_row), 2 * TILE)
            link = fact_next[piece][1:2].astype(jnp.int32)
            inside = (link >= HALO) & (link < HALO + TILE)
            row = jnp.where(inside, start * (TILE // HALO) + link - HALO, -1)
            pick_next[piece] = one_hot(row, width)
            return carry

        lax.fori_loop(0, pieces, one, 0)

    def prepare(sweep):
        loaded(sweep).wait()

        def one(level, piece):
            cols = columns_of(piece)
            value = product(local_weight[sweep], stacked(results[sweep][level, :, cols]))
            mask = live(level, piece)
            results[sweep][level, :, cols] = mask * value[:nodes]
            added = (mask if sweep == 0 else scale[level, piece, :, 0:width]) * value[nodes:]
            lead[sweep, level, piece, :, 0:width] = added
            if level == 0:
                lead[sweep, 0, piece, :, width:whole_width] = jnp.zeros((BOTH, TILE), F32)
                if sweep == 0:
                    start_out[piece] = packed(added[FACE:])

        def first_level(piece, carry):
            one(0, piece)
            return carry

        def second_level(piece, carry):
            one(1, piece)
            return carry

        lax.fori_loop(0, pieces, first_level, 0)
        if sweep == 0:
            start_all(start_copies())
        lax.fori_loop(0, pieces, second_level, 0)

    def arrive(sweep, piece):
        @pl.when(is_first[sweep])
        def _():
            main_in[sweep, piece] = jnp.zeros((BOTH, width), F32)
            near_left[sweep, piece] = jnp.zeros((NEAR, TILE), F32)
            near_right[sweep, piece] = jnp.zeros((NEAR, TILE), F32)
            far_left[sweep, piece] = jnp.zeros((FACE, TILE), F32)
            far_right[sweep, piece] = jnp.zeros((FACE, TILE), F32)

        @pl.when(jnp.logical_not(is_first[sweep]))
        def _():
            wait_received(wave_copies(sweep, piece))

    def leave(sweep, piece):
        start_all(wave_copies(sweep, piece))

    def picked(near, beyond, one_hots):
        near_high, near_low = near
        beyond_high, beyond_low = beyond
        extended = jnp.concatenate(
            [
                jnp.concatenate([near_high, beyond_high], axis=1),
                jnp.concatenate([near_low, beyond_low], axis=1),
            ],
            axis=0,
        )
        value = product(extended, one_hots)
        return value[:FACE] + value[FACE:]

    def spread(value, one_hots):
        value = cross_product(jnp.concatenate(halves(value), axis=0), one_hots)
        return value[:FACE] + value[FACE:]

    def cut(value, at):
        return value[:, at * TILE : (at + 1) * TILE]

    def gathered(sides, halo, level, piece):
        halo = halves(halo)
        high, low = halves(sides)
        return [
            picked((cut(high, at), cut(low, at)), halo, pick[level, piece * GROUP + at])
            for at in range(GROUP)
        ]

    def scattered(sides, level, piece):
        own = []
        edge = jnp.zeros((FACE, TILE), F32)
        for at in range(GROUP):
            value = spread(cut(sides, at), pick[level, piece * GROUP + at])
            own.append(value[:, :TILE])
            edge = edge + value[:, TILE:]
        return own, edge

    def forward(piece):
        arrive(0, piece)
        main = main_in[0, piece]
        near = inward(*unfolded(near_left[0, piece], near_right[0, piece]))
        outer = inward(far_left[0, piece], far_right[0, piece], 2)
        sides = gathered(main[FACE:], near[BOTH:], 0, piece)
        sides.append(
            near[FACE:BOTH]
            + picked(halves(packed(main[FACE:])), halves(outer), pick_beside[piece])
        )
        inbound = jnp.concatenate(
            [
                jnp.concatenate([main[:FACE], near[:FACE]], axis=1),
                jnp.concatenate(sides, axis=1),
            ],
            axis=0,
        )
        operand = stacked(inbound)
        kept[0, 0, piece] = operand[:, :width]
        value = lead[0, 0, piece] + scale[0, piece] * product(chain_weight[0], operand)
        sides = gathered(value[FACE:, :width], value[FACE:, width:], 1, piece)
        operand = stacked(
            jnp.concatenate([value[:FACE, :width], jnp.concatenate(sides, axis=1)], axis=0)
        )
        kept[0, 1, piece] = operand

        @pl.when(jnp.logical_not(is_last[0]))
        def _():
            value = lead[0, 1, piece, :, 0:width] + scale[1, piece, :, 0:width] * product(
                chain_weight[0], operand
            )
            edges = packed(value)
            ahead = product(jnp.concatenate(halves(value[FACE:]), axis=0), pick_next[piece])
            main_out[0, piece] = value
            near_out[0, piece, 0 : 3 * FACE] = folded(
                edges[:FACE], ahead[:FACE] + ahead[FACE:], edges[FACE:]
            )
            leave(0, piece)

    def adjoint(piece):
        arrive(1, piece)
        main = main_in[1, piece]
        highs, lows = near_left[1, piece], near_right[1, piece]
        near = homeward(*unfolded(lows, highs)[::-1])
        outer = homeward(far_left[1, piece], far_right[1, piece], 2)
        edges = jnp.concatenate(
            [near[:FACE], near[BOTH:] + outer], axis=0
        )
        behind = spread(near[FACE:BOTH], pick_next[piece])
        none = jnp.zeros((FACE, TILE), F32)
        inbound = jnp.concatenate(
            [
                cut(main, at)
                + unpacked(edges, at)
                + jnp.concatenate([none, cut(behind, at)], axis=0)
                for at in range(GROUP)
            ],
            axis=1,
        )
        operand = stacked(inbound)
        kept[1, 1, piece] = operand
        value = lead[1, 1, piece, :, 0:width] + scale[1, piece, :, 0:width] * product(
            chain_weight[1], operand
        )
        own, edge = scattered(value[FACE:], 1, piece)
        fix_out[piece] = edge
        start_all(fix_copies(piece))
        inbound = jnp.concatenate(
            [
                jnp.concatenate([value[:FACE], none], axis=1),
                jnp.concatenate(own + [edge], axis=1),
            ],
            axis=0,
        )
        late[piece] = inbound[:, :width]

        @pl.when(jnp.logical_not(is_last[1]))
        def _():
            value = lead[1, 0, piece] + scale[0, piece] * product(
                chain_weight[1], stacked(inbound)
            )
            own, edge = scattered(value[FACE:, :width], 0, piece)
            around = spread(value[FACE:, width:], pick_beside[piece])
            own = [own[at] + unpacked(around[:, :TILE], at) for at in range(GROUP)]
            main_out[1, piece, 0:FACE] = value[:FACE, :width]
            main_out[1, piece, FACE:BOTH] = jnp.concatenate(own, axis=1)
            near_out[1, piece, 0 : 3 * FACE] = folded(
                value[:FACE, width:], value[FACE:, width:], edge
            )
            near_out[1, piece, 3 * FACE : 4 * FACE] = around[:, TILE:]
            leave(1, piece)

    def finish(sweep, piece):
        cols = columns_of(piece)
        for level in range(LEVELS_HERE):
            if sweep == 1 and level == 0:
                wait_received(fix_copies(piece))
                edges = homeward(fix_left[piece], fix_right[piece])
                sides = [
                    cut(late[piece, FACE:BOTH], at) + unpacked(edges, at) for at in range(GROUP)
                ]
                operand = stacked(
                    jnp.concatenate(
                        [late[piece, 0:FACE], jnp.concatenate(sides, axis=1)], axis=0
                    )
                )
            else:
                operand = kept[sweep, level, piece]
            factor = scale[level, piece, :, 0:width] if sweep == 0 else live(level, piece)
            results[sweep][level, :, cols] += factor * product(out_weight[sweep], operand)

    def chain(sweep):
        step = forward if sweep == 0 else adjoint
        if sweep == 0:
            wait_received(start_copies())

            def begin(piece, carry):
                lead[0, 0, piece, FACE:BOTH, width:whole_width] = inward(
                    start_left[piece], start_right[piece]
                )
                return carry

            lax.fori_loop(0, pieces, begin, 0)

        def one(piece, carry):
            step(piece)
            return carry

        def last(piece, carry):
            finish(sweep, piece)
            return carry

        lax.fori_loop(0, pieces, one, 0)
        lax.fori_loop(0, pieces, last, 0)

    first = (place >= flow_count // 2).astype(jnp.int32)
    on_end = jnp.logical_or(place == 0, place == flow_count - 1)

    def slot(at, carry):
        early = jnp.where(on_end, 2 + first, 1 - first)
        late_op = jnp.where(on_end, 1 - first, 2 + first)
        op = jnp.where(
            at == 0, first, jnp.where(at == 1, early, jnp.where(at == 2, late_op, 3 - first))
        )

        @pl.when(op == 0)
        def _():
            prepare(0)

        @pl.when(op == 1)
        def _():
            prepare(1)

        @pl.when(at == 0)
        def _():
            settle_facts()

        @pl.when(op == 2)
        def _():
            chain(0)

        @pl.when(op == 3)
        def _():
            chain(1)

        return carry

    lax.fori_loop(0, 4, slot, 0)

    wait_sent(fact_copies() + start_copies())

    @pl.when(below)
    def _():
        wait_sent(next_copies())

    def settle(piece, carry):
        wait_sent(fix_copies(piece))
        for sweep in range(2):
            @pl.when(jnp.logical_not(is_last[sweep]))
            def _():
                wait_sent(wave_copies(sweep, piece))

        return carry

    lax.fori_loop(0, pieces, settle, 0)


def per_device(
    source,
    cotangent,
    flux,
    pore_mask,
    upwind,
    side_link,
    local_inverse,
    flow_lift,
    side_lift,
    flow_trace,
    side_trace,
):
    levels, nodes, elems = source.shape
    tiles = elems // TILE
    pieces = tiles // GROUP
    width = GROUP * TILE
    extended = width + TILE
    away = pl.BlockSpec(memory_space=pltpu.HBM)
    here = pl.BlockSpec(memory_space=pltpu.VMEM)
    dma = pltpu.SemaphoreType.DMA
    return pl.pallas_call(
        kernel,
        out_shape=(
            pltpu.VMEM(source.shape, F32),
            pltpu.VMEM(source.shape, F32),
        ),
        in_specs=[away] * 11,
        out_specs=(here, here),
        scratch_shapes=[
            pltpu.VMEM((2, levels, pieces, BOTH, extended), F32),
            pltpu.VMEM((levels, pieces, 1, extended), F32),
            pltpu.VMEM((levels, tiles, 2 * TILE, TILE), BF16),
            pltpu.VMEM((pieces, 2 * TILE, TILE), BF16),
            pltpu.VMEM((pieces, width, TILE), BF16),
            pltpu.VMEM((2, levels, pieces, 3 * BOTH, width), BF16),
            pltpu.VMEM((pieces, BOTH, width), F32),
            pltpu.VMEM((2, pieces, BOTH, width), F32),
            pltpu.VMEM((2, pieces, BOTH, width), F32),
            pltpu.VMEM((2, pieces, 4 * FACE, TILE), F32),
            pltpu.VMEM((2, pieces, NEAR, TILE), F32),
            pltpu.VMEM((2, pieces, NEAR, TILE), F32),
            pltpu.VMEM((2, pieces, FACE, TILE), F32),
            pltpu.VMEM((2, pieces, FACE, TILE), F32),
            pltpu.VMEM((pieces, FACE, TILE), F32),
            pltpu.VMEM((pieces, FACE, TILE), F32),
            pltpu.VMEM((pieces, FACE, TILE), F32),
            pltpu.VMEM((pieces, 8, TILE), F32),
            pltpu.VMEM((pieces, 8, TILE), F32),
            pltpu.VMEM((pieces, 8, TILE), F32),
            pltpu.VMEM((pieces, 8, TILE), F32),
            pltpu.VMEM((pieces, FACE, TILE), F32),
            pltpu.VMEM((pieces, FACE, TILE), F32),
            pltpu.VMEM((pieces, FACE, TILE), F32),
            pltpu.VMEM((levels, elems), F32),
            pltpu.VMEM((levels, elems), jnp.int32),
            pltpu.VMEM((levels, elems), jnp.int32),
            pltpu.VMEM((levels, elems), jnp.int32),
            pltpu.VMEM((nodes, nodes), F32),
            pltpu.VMEM((BOTH, nodes), F32),
            pltpu.VMEM((BOTH, nodes), F32),
            pltpu.VMEM((nodes + BOTH, 3 * nodes), F32),
            pltpu.VMEM((2, nodes + BOTH, 3 * nodes), BF16),
            pltpu.VMEM((2, BOTH, 3 * BOTH), BF16),
            pltpu.VMEM((2, nodes, 3 * BOTH), BF16),
            dma((9,)),
            dma((2,)),
            dma((2, 2, pieces)),
            dma((4, 2, pieces)),
            dma((4, 2, pieces)),
            dma((4, pieces)),
            dma((4,)),
            dma((2,)),
            dma((4,)),
        ],
        compiler_params=pltpu.CompilerParams(
            collective_id=0, has_side_effects=True, vmem_limit_bytes=LIMIT << 20
        ),
    )(
        *(
            pltpu.with_memory_space_constraint(operand, pltpu.HBM)
            for operand in (
                source,
                cotangent,
                flux,
                pore_mask,
                upwind,
                side_link,
                local_inverse,
                flow_lift.T,
                side_lift.T,
                flow_trace,
                side_trace,
            )
        )
    )


def solution(mesh):
    placed = (
        P("flow", None, "cross"),
        P("flow", None, "cross"),
        P("flow", "cross"),
        P("flow", "cross"),
        P("flow", "cross"),
        P("flow", "cross"),
        P(),
        P(),
        P(),
        P(),
        P(),
    )
    return jax.shard_map(
        per_device,
        mesh=mesh,
        in_specs=placed,
        out_specs=(P("flow", None, "cross"), P("flow", None, "cross")),
        check_vma=False,
    )
```

```python
import jax
import jax.numpy as jnp
from jax import lax
from jax.experimental import pallas as pl
from jax.experimental.pallas import tpu as pltpu
from jax.sharding import PartitionSpec as P

FACE = 16
TILE = 128
HALO = 16
LEVELS_HERE = 2
GROUP = 4
HALF = TILE // 2
BOTH = 2 * FACE
NEAR = 2 * FACE
LIMIT = 48

HIGH = lax.Precision.HIGHEST
F32 = jnp.float32
BF16 = jnp.bfloat16
MESH = pl.DeviceIdType.MESH


def halves(value):
    high = value.astype(BF16)
    low = (value - high.astype(F32)).astype(BF16)
    return high, low


def stacked(value):
    high, low = halves(value)
    return jnp.concatenate([high, low, high], axis=0)


def product(left, right):
    return jnp.dot(left, right, preferred_element_type=F32)


def cross_product(left, right):
    return lax.dot_general(left, right, (((1,), (1,)), ((), ())), preferred_element_type=F32)


def widened(weight, wide, target):
    depth = weight.shape[1]
    high = weight.astype(BF16).astype(F32)
    wide[0 : weight.shape[0], 0:depth] = high
    wide[0 : weight.shape[0], depth : 2 * depth] = high
    wide[0 : weight.shape[0], 2 * depth : 3 * depth] = weight - high
    target[...] = wide[0 : weight.shape[0], 0 : 3 * depth].astype(BF16)


def kernel(
    source,
    cotangent,
    flux_away,
    pore_mask_away,
    upwind_away,
    side_link_away,
    local_inverse_away,
    flow_lift_rows,
    side_lift_rows,
    flow_trace,
    side_trace,
    concentration,
    sensitivity,
    lead,
    scale,
    pick,
    pick_beside,
    pick_next,
    kept,
    late,
    main_in,
    main_out,
    near_out,
    near_left,
    near_right,
    far_left,
    far_right,
    fix_out,
    fix_left,
    fix_right,
    fact_out,
    fact_left,
    fact_right,
    fact_next,
    start_out,
    start_left,
    start_right,
    flux,
    pore_mask,
    upwind,
    side_link,
    local_inverse,
    lift_rows,
    trace_rows,
    wide,
    local_weight,
    chain_weight,
    out_weight,
    small_sem,
    field_sem,
    main_sem,
    near_sem,
    far_sem,
    fix_sem,
    fact_sem,
    next_sem,
    start_sem,
):
    flow_count = lax.axis_size("flow")
    cross_count = lax.axis_size("cross")
    place = lax.axis_index("flow")
    block = lax.axis_index("cross")
    pieces = main_in.shape[1]
    width = main_in.shape[3]
    whole_width = width + TILE
    nodes = concentration.shape[1]
    inputs = (source, cotangent)
    results = (concentration, sensitivity)
    is_first = (place == 0, place == flow_count - 1)
    is_last = (place == flow_count - 1, place == 0)
    downstream = (place + 1, place - 1)
    below, above = place > 0, place < flow_count - 1

    def inside(steps):
        return (block + steps >= 0) & (block + steps < cross_count)

    def loaded(sweep):
        return pltpu.make_async_copy(inputs[sweep], results[sweep], field_sem.at[sweep])

    small = (
        (side_link_away, side_link),
        (upwind_away, upwind),
        (flux_away, flux),
        (pore_mask_away, pore_mask),
        (local_inverse_away, local_inverse),
        (flow_trace, trace_rows.at[pl.ds(0, FACE)]),
        (side_trace, trace_rows.at[pl.ds(FACE, FACE)]),
        (flow_lift_rows, lift_rows.at[pl.ds(0, FACE)]),
        (side_lift_rows, lift_rows.at[pl.ds(FACE, FACE)]),
    )
    fetches = [
        pltpu.make_async_copy(src, dst, small_sem.at[n]) for n, (src, dst) in enumerate(small)
    ]
    for fetch in fetches:
        fetch.start()

    @pl.when(above)
    def _():
        loaded(0).start()
        loaded(1).start()

    @pl.when(jnp.logical_not(above))
    def _():
        loaded(1).start()
        loaded(0).start()

    barrier = pltpu.get_barrier_semaphore()

    def greet(flow_at, steps):
        @pl.when(inside(steps))
        def _():
            pl.semaphore_signal(
                barrier, inc=1, device_id=(flow_at, block + steps), device_id_type=MESH
            )

    greet(place, -1)
    greet(place, 1)

    @pl.when(below)
    def _():
        for steps in range(-2, 3):
            greet(place - 1, steps)

    @pl.when(above)
    def _():
        for steps in range(-2, 3):
            greet(place + 1, steps)

    in_line = [inside(steps).astype(jnp.int32) for steps in range(-2, 3)]
    met = (below.astype(jnp.int32) + above.astype(jnp.int32)) * sum(in_line)
    met = met + in_line[1] + in_line[3]

    for fetch in fetches:
        fetch.wait()

    inverse = local_inverse[...]
    lifts = lift_rows[...].T
    trace = trace_rows[...]
    traced_inverse = jnp.dot(trace, inverse, precision=HIGH, preferred_element_type=F32)
    traced_lift = jnp.dot(trace, lifts, precision=HIGH, preferred_element_type=F32)
    widened(jnp.concatenate([inverse, traced_inverse], axis=0), wide, local_weight.at[0])
    widened(jnp.concatenate([inverse.T, lift_rows[...]], axis=0), wide, local_weight.at[1])
    widened(traced_lift, wide, chain_weight.at[0])
    widened(traced_lift.T, wide, chain_weight.at[1])
    widened(lifts, wide, out_weight.at[0])
    widened(traced_inverse.T, wide, out_weight.at[1])

    def lanes(rows):
        return lax.broadcasted_iota(jnp.int32, (rows, TILE), 1)

    def packed(value):
        lane = lanes(value.shape[0])
        edge = jnp.zeros(lane.shape, F32)
        for at in range(GROUP):
            tile = value[:, at * TILE : (at + 1) * TILE]
            start = at * HALO
            tail = pltpu.roll(tile, (start + HALO) % TILE, 1)
            head = pltpu.roll(tile, (start + HALF) % TILE, 1)
            edge = jnp.where((lane >= start) & (lane < start + HALO), tail, edge)
            edge = jnp.where((lane >= start + HALF) & (lane < start + HALF + HALO), head, edge)
        return edge

    def unpacked(edge, at):
        lane = lanes(edge.shape[0])
        start = at * HALO
        head = pltpu.roll(edge, (TILE - HALF - start) % TILE, 1)
        tail = pltpu.roll(edge, (TILE - HALO - start) % TILE, 1)
        return jnp.where(lane < HALO, head, jnp.where(lane >= TILE - HALO, tail, 0.0))

    def is_open(reach):
        return (
            (block >= reach).astype(jnp.int32),
            (block < cross_count - reach).astype(jnp.int32),
        )

    def inward(from_left, from_right, reach=1):
        lane = lanes(from_left.shape[0])
        opened = jnp.where(lane < HALF, *is_open(reach))
        return jnp.where(opened > 0, jnp.where(lane < HALF, from_left, from_right), 0.0)

    def homeward(from_left, from_right, reach=1):
        lane = lanes(from_left.shape[0])
        opened = jnp.where(lane < HALF, *is_open(reach)[::-1])
        return jnp.where(opened > 0, jnp.where(lane < HALF, from_right, from_left), 0.0)

    def swapped(value):
        return pltpu.roll(value, HALF, 1)

    def folded(first, second):
        lane = lanes(FACE)
        low = jnp.where(lane < HALF, first, swapped(second))
        high = jnp.where(lane < HALF, swapped(first), second)
        return low, high

    def unfolded(lows, highs):
        low = jnp.concatenate([lows[:FACE], swapped(lows[:FACE]), lows[FACE:]], axis=0)
        high = jnp.concatenate([swapped(highs[FACE:]), highs[FACE:], highs[:FACE]], axis=0)
        return low, high

    def columns_of(piece):
        return pl.ds(pl.multiple_of(piece * width, width), width)

    def live(level, piece):
        return pore_mask[level : level + 1, columns_of(piece)].astype(F32)

    def codes(level, piece):
        cols = columns_of(piece)
        inflow = upwind[level : level + 1, cols]
        return jnp.where(inflow != 0, side_link[level : level + 1, cols], -1)

    def gather_facts(piece, carry):
        for level in range(LEVELS_HERE):
            cols = columns_of(piece)
            scale[level, piece, :, 0:width] = live(level, piece) * flux[level : level + 1, cols]
        rows = jnp.concatenate(
            [
                scale[0, piece, :, 0:width],
                codes(0, piece).astype(F32),
                jnp.zeros((6, width), F32),
            ],
            axis=0,
        )
        fact_out[piece] = packed(rows)
        return carry

    lax.fori_loop(0, pieces, gather_facts, 0)

    def send(src, dst, send_sem, recv_sem, flow_at, steps):
        copy = pltpu.make_async_remote_copy(
            src_ref=src,
            dst_ref=dst,
            send_sem=send_sem,
            recv_sem=recv_sem,
            device_id=(flow_at, block + steps),
            device_id_type=MESH,
        )
        return copy, steps

    def pair(src, at_left, at_right, sem, flow_at, reach=1):
        return (
            send(src, at_left, sem(0), sem(1), flow_at, reach),
            send(src, at_right, sem(2), sem(3), flow_at, -reach),
        )

    def each(copies, act, sign):
        for copy, steps in copies:
            if steps == 0:
                act(copy)
            else:
                pl.when(inside(sign * steps))(lambda copy=copy: act(copy))

    def start_all(copies):
        each(copies, lambda copy: copy.start(), 1)

    def wait_sent(copies):
        each(copies, lambda copy: copy.wait_send(), 1)

    def wait_received(copies):
        each(copies, lambda copy: copy.wait_recv(), -1)

    def fact_copies():
        return pair(fact_out, fact_left, fact_right, lambda n: fact_sem.at[n], place)

    def next_copies():
        return (send(fact_out, fact_next, next_sem.at[0], next_sem.at[1], place - 1, 0),)

    def start_copies():
        return pair(start_out, start_left, start_right, lambda n: start_sem.at[n], place)

    def fix_copies(piece):
        return pair(
            fix_out.at[piece],
            fix_left.at[piece],
            fix_right.at[piece],
            lambda n: fix_sem.at[n, piece],
            place,
        )

    def wave_copies(sweep, piece):
        flow_at = downstream[sweep]
        main = send(
            main_out.at[sweep, piece],
            main_in.at[sweep, piece],
            main_sem.at[0, sweep, piece],
            main_sem.at[1, sweep, piece],
            flow_at,
            0,
        )
        low = near_out.at[sweep, piece, pl.ds(0, NEAR)]
        high = near_out.at[sweep, piece, pl.ds(FACE, NEAR)]
        ahead, back = (low, high) if sweep == 0 else (high, low)
        near = (
            send(
                ahead,
                near_left.at[sweep, piece],
                near_sem.at[0, sweep, piece],
                near_sem.at[1, sweep, piece],
                flow_at,
                1,
            ),
            send(
                back,
                near_right.at[sweep, piece],
                near_sem.at[2, sweep, piece],
                near_sem.at[3, sweep, piece],
                flow_at,
                -1,
            ),
        )
        far = pair(
            near_out.at[sweep, piece, pl.ds(FACE if sweep == 0 else 3 * FACE, FACE)],
            far_left.at[sweep, piece],
            far_right.at[sweep, piece],
            lambda n: far_sem.at[n, sweep, piece],
            flow_at,
            2,
        )
        return far + near + (main,)

    pl.semaphore_wait(barrier, met)

    start_all(fact_copies())

    @pl.when(below)
    def _():
        start_all(next_copies())

    def one_hot(row, depth):
        rows = lax.broadcasted_iota(jnp.int32, (depth, TILE), 0)
        return jnp.where(rows == row, 1.0, 0.0).astype(BF16)

    def build_pick(piece, carry):
        for level in range(LEVELS_HERE):
            code = codes(level, piece)
            for at in range(GROUP):
                link = code[:, at * TILE : (at + 1) * TILE]
                row = jnp.where(
                    link < HALO,
                    link + (TILE + at * HALO),
                    jnp.where(
                        link < HALO + TILE, link - HALO, link + (HALF + at * HALO - HALO)
                    ),
                )
                row = jnp.where(link >= 0, row, -1)
                pick[level, piece * GROUP + at] = one_hot(row, 2 * TILE)
        return carry

    lax.fori_loop(0, pieces, build_pick, 0)

    def settle_facts():
        wait_received(fact_copies())

        @pl.when(above)
        def _():
            wait_received(next_copies())

        @pl.when(jnp.logical_not(above))
        def _():
            fact_next[...] = jnp.zeros(fact_next.shape, F32)

        lane = lanes(1)
        start = lax.rem(lane, HALF) // HALO * HALO
        on_left = lane < HALF

        def one(piece, carry):
            facts = inward(fact_left[piece], fact_right[piece])
            scale[0, piece, :, width:whole_width] = facts[0:1]
            link = facts[1:2].astype(jnp.int32)
            low = (link >= 0) & (link < HALO)
            high = link >= HALO + TILE
            after = link - (HALO + TILE)
            left_row = jnp.where(
                high, HALF + start + after, jnp.where(low, TILE + start + link, -1)
            )
            right_row = jnp.where(
                low, start + link, jnp.where(high, TILE + HALF + start + after, -1)
            )
            pick_beside[piece] = one_hot(jnp.where(on_left, left_row, right_row), 2 * TILE)
            link = fact_next[piece][1:2].astype(jnp.int32)
            inside = (link >= HALO) & (link < HALO + TILE)
            row = jnp.where(inside, start * (TILE // HALO) + link - HALO, -1)
            pick_next[piece] = one_hot(row, width)
            return carry

        lax.fori_loop(0, pieces, one, 0)

    def prepare(sweep):
        loaded(sweep).wait()

        def one(level, piece):
            cols = columns_of(piece)
            value = product(local_weight[sweep], stacked(results[sweep][level, :, cols]))
            mask = live(level, piece)
            results[sweep][level, :, cols] = mask * value[:nodes]
            added = (mask if sweep == 0 else scale[level, piece, :, 0:width]) * value[nodes:]
            lead[sweep, level, piece, :, 0:width] = added
            if level == 0:
                lead[sweep, 0, piece, :, width:whole_width] = jnp.zeros((BOTH, TILE), F32)
                if sweep == 0:
                    start_out[piece] = packed(added[FACE:])

        def first_level(piece, carry):
            one(0, piece)
            return carry

        def second_level(piece, carry):
            one(1, piece)
            return carry

        lax.fori_loop(0, pieces, first_level, 0)
        if sweep == 0:
            start_all(start_copies())
        lax.fori_loop(0, pieces, second_level, 0)

    def arrive(sweep, piece):
        @pl.when(is_first[sweep])
        def _():
            main_in[sweep, piece] = jnp.zeros((BOTH, width), F32)
            near_left[sweep, piece] = jnp.zeros((NEAR, TILE), F32)
            near_right[sweep, piece] = jnp.zeros((NEAR, TILE), F32)
            far_left[sweep, piece] = jnp.zeros((FACE, TILE), F32)
            far_right[sweep, piece] = jnp.zeros((FACE, TILE), F32)

        @pl.when(jnp.logical_not(is_first[sweep]))
        def _():
            wait_received(wave_copies(sweep, piece))

    def leave_far(sweep, piece):
        start_all(wave_copies(sweep, piece)[:2])

    def leave(sweep, piece):
        start_all(wave_copies(sweep, piece)[2:])

    def picked(near, beyond, one_hots):
        near_high, near_low = near
        beyond_high, beyond_low = beyond
        extended = jnp.concatenate(
            [
                jnp.concatenate([near_high, beyond_high], axis=1),
                jnp.concatenate([near_low, beyond_low], axis=1),
            ],
            axis=0,
        )
        value = product(extended, one_hots)
        return value[:FACE] + value[FACE:]

    def spread(value, one_hots):
        value = cross_product(jnp.concatenate(halves(value), axis=0), one_hots)
        return value[:FACE] + value[FACE:]

    def cut(value, at):
        return value[:, at * TILE : (at + 1) * TILE]

    def gathered(sides, halo, level, piece):
        halo = halves(halo)
        high, low = halves(sides)
        return [
            picked((cut(high, at), cut(low, at)), halo, pick[level, piece * GROUP + at])
            for at in range(GROUP)
        ]

    def scattered(sides, level, piece):
        own = []
        edge = jnp.zeros((FACE, TILE), F32)
        for at in range(GROUP):
            value = spread(cut(sides, at), pick[level, piece * GROUP + at])
            own.append(value[:, :TILE])
            edge = edge + value[:, TILE:]
        return own, edge

    def forward(piece):
        arrive(0, piece)
        main = main_in[0, piece]
        near = inward(*unfolded(near_left[0, piece], near_right[0, piece]))
        outer = inward(far_left[0, piece], far_right[0, piece], 2)
        sides = gathered(main[FACE:], near[BOTH:], 0, piece)
        sides.append(
            near[FACE:BOTH]
            + picked(halves(packed(main[FACE:])), halves(outer), pick_beside[piece])
        )
        inbound = jnp.concatenate(
            [
                jnp.concatenate([main[:FACE], near[:FACE]], axis=1),
                jnp.concatenate(sides, axis=1),
            ],
            axis=0,
        )
        operand = stacked(inbound)
        kept[0, 0, piece] = operand[:, :width]
        value = lead[0, 0, piece] + scale[0, piece] * product(chain_weight[0], operand)
        sides = gathered(value[FACE:, :width], value[FACE:, width:], 1, piece)
        operand = stacked(
            jnp.concatenate([value[:FACE, :width], jnp.concatenate(sides, axis=1)], axis=0)
        )
        kept[0, 1, piece] = operand

        @pl.when(jnp.logical_not(is_last[0]))
        def _():
            value = lead[0, 1, piece, :, 0:width] + scale[1, piece, :, 0:width] * product(
                chain_weight[0], operand
            )
            edges = packed(value)
            near_out[0, piece, FACE : 2 * FACE] = edges[FACE:]
            leave_far(0, piece)
            ahead = product(jnp.concatenate(halves(value[FACE:]), axis=0), pick_next[piece])
            main_out[0, piece] = value
            low, high = folded(edges[:FACE], ahead[:FACE] + ahead[FACE:])
            near_out[0, piece, 0:FACE] = low
            near_out[0, piece, 2 * FACE : 3 * FACE] = high
            leave(0, piece)

    def adjoint(piece):
        arrive(1, piece)
        main = main_in[1, piece]
        highs, lows = near_left[1, piece], near_right[1, piece]
        near = homeward(*unfolded(lows, highs)[::-1])
        outer = homeward(far_left[1, piece], far_right[1, piece], 2)
        edges = jnp.concatenate(
            [near[:FACE], near[BOTH:] + outer], axis=0
        )
        behind = spread(near[FACE:BOTH], pick_next[piece])
        none = jnp.zeros((FACE, TILE), F32)
        inbound = jnp.concatenate(
            [
                cut(main, at)
                + unpacked(edges, at)
                + jnp.concatenate([none, cut(behind, at)], axis=0)
                for at in range(GROUP)
            ],
            axis=1,
        )
        operand = stacked(inbound)
        kept[1, 1, piece] = operand
        value = lead[1, 1, piece, :, 0:width] + scale[1, piece, :, 0:width] * product(
            chain_weight[1], operand
        )
        own, edge = scattered(value[FACE:], 1, piece)
        fix_out[piece] = edge
        inbound = jnp.concatenate(
            [
                jnp.concatenate([value[:FACE], none], axis=1),
                jnp.concatenate(own + [edge], axis=1),
            ],
            axis=0,
        )
        late[piece] = inbound[:, :width]

        @pl.when(jnp.logical_not(is_last[1]))
        def _():
            value = lead[1, 0, piece] + scale[0, piece] * product(
                chain_weight[1], stacked(inbound)
            )
            around = spread(value[FACE:, width:], pick_beside[piece])
            near_out[1, piece, 3 * FACE : 4 * FACE] = around[:, TILE:]
            leave_far(1, piece)
            own, edge = scattered(value[FACE:, :width], 0, piece)
            own = [own[at] + unpacked(around[:, :TILE], at) for at in range(GROUP)]
            main_out[1, piece, 0:FACE] = value[:FACE, :width]
            main_out[1, piece, FACE:BOTH] = jnp.concatenate(own, axis=1)
            low, high = folded(value[:FACE, width:], value[FACE:, width:])
            near_out[1, piece, 0:FACE] = low
            near_out[1, piece, FACE : 2 * FACE] = edge
            near_out[1, piece, 2 * FACE : 3 * FACE] = high
            leave(1, piece)

        start_all(fix_copies(piece))

    def finish(sweep, level, piece):
        cols = columns_of(piece)
        if sweep == 1 and level == 0:
            wait_received(fix_copies(piece))
            edges = homeward(fix_left[piece], fix_right[piece])
            sides = [
                cut(late[piece, FACE:BOTH], at) + unpacked(edges, at) for at in range(GROUP)
            ]
            operand = stacked(
                jnp.concatenate([late[piece, 0:FACE], jnp.concatenate(sides, axis=1)], axis=0)
            )
        else:
            operand = kept[sweep, level, piece]
        factor = scale[level, piece, :, 0:width] if sweep == 0 else live(level, piece)
        results[sweep][level, :, cols] += factor * product(out_weight[sweep], operand)

    def chain(sweep):
        step = forward if sweep == 0 else adjoint
        if sweep == 0:
            wait_received(start_copies())

            def begin(piece, carry):
                lead[0, 0, piece, FACE:BOTH, width:whole_width] = inward(
                    start_left[piece], start_right[piece]
                )
                return carry

            lax.fori_loop(0, pieces, begin, 0)

        def one(piece, carry):
            step(piece)
            return carry

        def upper(piece, carry):
            finish(sweep, 1, piece)
            return carry

        def last(piece, carry):
            finish(sweep, 0, piece)
            return carry

        lax.fori_loop(0, pieces, one, 0)
        lax.fori_loop(0, pieces, upper, 0)
        lax.fori_loop(0, pieces, last, 0)

    first = (place >= flow_count // 2).astype(jnp.int32)
    on_end = jnp.logical_or(place == 0, place == flow_count - 1)

    def slot(at, carry):
        early = jnp.where(on_end, 2 + first, 1 - first)
        late_op = jnp.where(on_end, 1 - first, 2 + first)
        op = jnp.where(
            at == 0, first, jnp.where(at == 1, early, jnp.where(at == 2, late_op, 3 - first))
        )

        @pl.when(op == 0)
        def _():
            prepare(0)

        @pl.when(op == 1)
        def _():
            prepare(1)

        @pl.when(at == 0)
        def _():
            settle_facts()

        @pl.when(op == 2)
        def _():
            chain(0)

        @pl.when(op == 3)
        def _():
            chain(1)

        return carry

    lax.fori_loop(0, 4, slot, 0)

    wait_sent(fact_copies() + start_copies())

    @pl.when(below)
    def _():
        wait_sent(next_copies())

    def settle(piece, carry):
        wait_sent(fix_copies(piece))
        for sweep in range(2):
            @pl.when(jnp.logical_not(is_last[sweep]))
            def _():
                wait_sent(wave_copies(sweep, piece))

        return carry

    lax.fori_loop(0, pieces, settle, 0)


def per_device(
    source,
    cotangent,
    flux,
    pore_mask,
    upwind,
    side_link,
    local_inverse,
    flow_lift,
    side_lift,
    flow_trace,
    side_trace,
):
    levels, nodes, elems = source.shape
    tiles = elems // TILE
    pieces = tiles // GROUP
    width = GROUP * TILE
    extended = width + TILE
    away = pl.BlockSpec(memory_space=pltpu.HBM)
    here = pl.BlockSpec(memory_space=pltpu.VMEM)
    dma = pltpu.SemaphoreType.DMA
    return pl.pallas_call(
        kernel,
        out_shape=(
            pltpu.VMEM(source.shape, F32),
            pltpu.VMEM(source.shape, F32),
        ),
        in_specs=[away] * 11,
        out_specs=(here, here),
        scratch_shapes=[
            pltpu.VMEM((2, levels, pieces, BOTH, extended), F32),
            pltpu.VMEM((levels, pieces, 1, extended), F32),
            pltpu.VMEM((levels, tiles, 2 * TILE, TILE), BF16),
            pltpu.VMEM((pieces, 2 * TILE, TILE), BF16),
            pltpu.VMEM((pieces, width, TILE), BF16),
            pltpu.VMEM((2, levels, pieces, 3 * BOTH, width), BF16),
            pltpu.VMEM((pieces, BOTH, width), F32),
            pltpu.VMEM((2, pieces, BOTH, width), F32),
            pltpu.VMEM((2, pieces, BOTH, width), F32),
            pltpu.VMEM((2, pieces, 4 * FACE, TILE), F32),
            pltpu.VMEM((2, pieces, NEAR, TILE), F32),
            pltpu.VMEM((2, pieces, NEAR, TILE), F32),
            pltpu.VMEM((2, pieces, FACE, TILE), F32),
            pltpu.VMEM((2, pieces, FACE, TILE), F32),
            pltpu.VMEM((pieces, FACE, TILE), F32),
            pltpu.VMEM((pieces, FACE, TILE), F32),
            pltpu.VMEM((pieces, FACE, TILE), F32),
            pltpu.VMEM((pieces, 8, TILE), F32),
            pltpu.VMEM((pieces, 8, TILE), F32),
            pltpu.VMEM((pieces, 8, TILE), F32),
            pltpu.VMEM((pieces, 8, TILE), F32),
            pltpu.VMEM((pieces, FACE, TILE), F32),
            pltpu.VMEM((pieces, FACE, TILE), F32),
            pltpu.VMEM((pieces, FACE, TILE), F32),
            pltpu.VMEM((levels, elems), F32),
            pltpu.VMEM((levels, elems), jnp.int32),
            pltpu.VMEM((levels, elems), jnp.int32),
            pltpu.VMEM((levels, elems), jnp.int32),
            pltpu.VMEM((nodes, nodes), F32),
            pltpu.VMEM((BOTH, nodes), F32),
            pltpu.VMEM((BOTH, nodes), F32),
            pltpu.VMEM((nodes + BOTH, 3 * nodes), F32),
            pltpu.VMEM((2, nodes + BOTH, 3 * nodes), BF16),
            pltpu.VMEM((2, BOTH, 3 * BOTH), BF16),
            pltpu.VMEM((2, nodes, 3 * BOTH), BF16),
            dma((9,)),
            dma((2,)),
            dma((2, 2, pieces)),
            dma((4, 2, pieces)),
            dma((4, 2, pieces)),
            dma((4, pieces)),
            dma((4,)),
            dma((2,)),
            dma((4,)),
        ],
        compiler_params=pltpu.CompilerParams(
            collective_id=0, has_side_effects=True, vmem_limit_bytes=LIMIT << 20
        ),
    )(
        *(
            pltpu.with_memory_space_constraint(operand, pltpu.HBM)
            for operand in (
                source,
                cotangent,
                flux,
                pore_mask,
                upwind,
                side_link,
                local_inverse,
                flow_lift.T,
                side_lift.T,
                flow_trace,
                side_trace,
            )
        )
    )


def solution(mesh):
    placed = (
        P("flow", None, "cross"),
        P("flow", None, "cross"),
        P("flow", "cross"),
        P("flow", "cross"),
        P("flow", "cross"),
        P("flow", "cross"),
        P(),
        P(),
        P(),
        P(),
        P(),
    )
    return jax.shard_map(
        per_device,
        mesh=mesh,
        in_specs=placed,
        out_specs=(P("flow", None, "cross"), P("flow", None, "cross")),
        check_vma=False,
    )
```

```python
import jax
import jax.numpy as jnp
from jax import lax
from jax.experimental import pallas as pl
from jax.experimental.pallas import tpu as pltpu
from jax.sharding import PartitionSpec as P

FACE = 16
TILE = 128
HALO = 16
LEVELS_HERE = 2
GROUP = 4
HALF = TILE // 2
BOTH = 2 * FACE
NEAR = 2 * FACE
LIMIT = 48

HIGH = lax.Precision.HIGHEST
F32 = jnp.float32
BF16 = jnp.bfloat16
MESH = pl.DeviceIdType.MESH


def halves(value):
    high = value.astype(BF16)
    low = (value - high.astype(F32)).astype(BF16)
    return high, low


def stacked(value):
    high, low = halves(value)
    return jnp.concatenate([high, low, high], axis=0)


def product(left, right):
    return jnp.dot(left, right, preferred_element_type=F32)


def cross_product(left, right):
    return lax.dot_general(left, right, (((1,), (1,)), ((), ())), preferred_element_type=F32)


def widened(weight, wide, target):
    depth = weight.shape[1]
    high = weight.astype(BF16).astype(F32)
    wide[0 : weight.shape[0], 0:depth] = high
    wide[0 : weight.shape[0], depth : 2 * depth] = high
    wide[0 : weight.shape[0], 2 * depth : 3 * depth] = weight - high
    target[...] = wide[0 : weight.shape[0], 0 : 3 * depth].astype(BF16)


def kernel(
    source,
    cotangent,
    flux_away,
    pore_mask_away,
    upwind_away,
    side_link_away,
    local_inverse_away,
    flow_lift_rows,
    side_lift_rows,
    flow_trace,
    side_trace,
    concentration,
    sensitivity,
    lead,
    scale,
    pick,
    pick_beside,
    pick_next,
    kept,
    late,
    main_in,
    main_out,
    near_out,
    near_left,
    near_right,
    far_left,
    far_right,
    fix_out,
    fix_left,
    fix_right,
    fact_out,
    fact_left,
    fact_right,
    fact_next,
    start_out,
    start_left,
    start_right,
    flux,
    pore_mask,
    upwind,
    side_link,
    local_inverse,
    lift_rows,
    trace_rows,
    wide,
    local_weight,
    chain_weight,
    out_weight,
    small_sem,
    field_sem,
    main_sem,
    near_sem,
    far_sem,
    fix_sem,
    fact_sem,
    next_sem,
    start_sem,
):
    flow_count = lax.axis_size("flow")
    cross_count = lax.axis_size("cross")
    place = lax.axis_index("flow")
    block = lax.axis_index("cross")
    pieces = main_in.shape[1]
    width = main_in.shape[3]
    whole_width = width + TILE
    nodes = concentration.shape[1]
    inputs = (source, cotangent)
    results = (concentration, sensitivity)
    is_first = (place == 0, place == flow_count - 1)
    is_last = (place == flow_count - 1, place == 0)
    downstream = (place + 1, place - 1)
    below, above = place > 0, place < flow_count - 1

    def inside(steps):
        return (block + steps >= 0) & (block + steps < cross_count)

    def loaded(sweep):
        return pltpu.make_async_copy(inputs[sweep], results[sweep], field_sem.at[sweep])

    small = (
        (side_link_away, side_link),
        (upwind_away, upwind),
        (flux_away, flux),
        (pore_mask_away, pore_mask),
        (local_inverse_away, local_inverse),
        (flow_trace, trace_rows.at[pl.ds(0, FACE)]),
        (side_trace, trace_rows.at[pl.ds(FACE, FACE)]),
        (flow_lift_rows, lift_rows.at[pl.ds(0, FACE)]),
        (side_lift_rows, lift_rows.at[pl.ds(FACE, FACE)]),
    )
    fetches = [
        pltpu.make_async_copy(src, dst, small_sem.at[n]) for n, (src, dst) in enumerate(small)
    ]
    for fetch in fetches:
        fetch.start()

    @pl.when(above)
    def _():
        loaded(0).start()
        loaded(1).start()

    @pl.when(jnp.logical_not(above))
    def _():
        loaded(1).start()
        loaded(0).start()

    barrier = pltpu.get_barrier_semaphore()

    def greet(flow_at, steps):
        @pl.when(inside(steps))
        def _():
            pl.semaphore_signal(
                barrier, inc=1, device_id=(flow_at, block + steps), device_id_type=MESH
            )

    greet(place, -1)
    greet(place, 1)

    @pl.when(below)
    def _():
        for steps in range(-2, 3):
            greet(place - 1, steps)

    @pl.when(above)
    def _():
        for steps in range(-2, 3):
            greet(place + 1, steps)

    in_line = [inside(steps).astype(jnp.int32) for steps in range(-2, 3)]
    met = (below.astype(jnp.int32) + above.astype(jnp.int32)) * sum(in_line)
    met = met + in_line[1] + in_line[3]

    for fetch in fetches[:4]:
        fetch.wait()

    def lanes(rows):
        return lax.broadcasted_iota(jnp.int32, (rows, TILE), 1)

    def packed(value):
        lane = lanes(value.shape[0])
        edge = jnp.zeros(lane.shape, F32)
        for at in range(GROUP):
            tile = value[:, at * TILE : (at + 1) * TILE]
            start = at * HALO
            tail = pltpu.roll(tile, (start + HALO) % TILE, 1)
            head = pltpu.roll(tile, (start + HALF) % TILE, 1)
            edge = jnp.where((lane >= start) & (lane < start + HALO), tail, edge)
            edge = jnp.where((lane >= start + HALF) & (lane < start + HALF + HALO), head, edge)
        return edge

    def unpacked(edge, at):
        lane = lanes(edge.shape[0])
        start = at * HALO
        head = pltpu.roll(edge, (TILE - HALF - start) % TILE, 1)
        tail = pltpu.roll(edge, (TILE - HALO - start) % TILE, 1)
        return jnp.where(lane < HALO, head, jnp.where(lane >= TILE - HALO, tail, 0.0))

    def is_open(reach):
        return (
            (block >= reach).astype(jnp.int32),
            (block < cross_count - reach).astype(jnp.int32),
        )

    def inward(from_left, from_right, reach=1):
        lane = lanes(from_left.shape[0])
        opened = jnp.where(lane < HALF, *is_open(reach))
        return jnp.where(opened > 0, jnp.where(lane < HALF, from_left, from_right), 0.0)

    def homeward(from_left, from_right, reach=1):
        lane = lanes(from_left.shape[0])
        opened = jnp.where(lane < HALF, *is_open(reach)[::-1])
        return jnp.where(opened > 0, jnp.where(lane < HALF, from_right, from_left), 0.0)

    def swapped(value):
        return pltpu.roll(value, HALF, 1)

    def folded(first, second):
        lane = lanes(FACE)
        low = jnp.where(lane < HALF, first, swapped(second))
        high = jnp.where(lane < HALF, swapped(first), second)
        return low, high

    def unfolded(lows, highs):
        low = jnp.concatenate([lows[:FACE], swapped(lows[:FACE]), lows[FACE:]], axis=0)
        high = jnp.concatenate([swapped(highs[FACE:]), highs[FACE:], highs[:FACE]], axis=0)
        return low, high

    def columns_of(piece):
        return pl.ds(pl.multiple_of(piece * width, width), width)

    def live(level, piece):
        return pore_mask[level : level + 1, columns_of(piece)].astype(F32)

    def codes(level, piece):
        cols = columns_of(piece)
        inflow = upwind[level : level + 1, cols]
        return jnp.where(inflow != 0, side_link[level : level + 1, cols], -1)

    def gather_facts(piece, carry):
        for level in range(LEVELS_HERE):
            cols = columns_of(piece)
            scale[level, piece, :, 0:width] = live(level, piece) * flux[level : level + 1, cols]
        rows = jnp.concatenate(
            [
                scale[0, piece, :, 0:width],
                codes(0, piece).astype(F32),
                jnp.zeros((6, width), F32),
            ],
            axis=0,
        )
        fact_out[piece] = packed(rows)
        return carry

    lax.fori_loop(0, pieces, gather_facts, 0)

    def send(src, dst, send_sem, recv_sem, flow_at, steps):
        copy = pltpu.make_async_remote_copy(
            src_ref=src,
            dst_ref=dst,
            send_sem=send_sem,
            recv_sem=recv_sem,
            device_id=(flow_at, block + steps),
            device_id_type=MESH,
        )
        return copy, steps

    def pair(src, at_left, at_right, sem, flow_at, reach=1):
        return (
            send(src, at_left, sem(0), sem(1), flow_at, reach),
            send(src, at_right, sem(2), sem(3), flow_at, -reach),
        )

    def each(copies, act, sign):
        for copy, steps in copies:
            if steps == 0:
                act(copy)
            else:
                pl.when(inside(sign * steps))(lambda copy=copy: act(copy))

    def start_all(copies):
        each(copies, lambda copy: copy.start(), 1)

    def wait_sent(copies):
        each(copies, lambda copy: copy.wait_send(), 1)

    def wait_received(copies):
        each(copies, lambda copy: copy.wait_recv(), -1)

    def fact_copies():
        return pair(fact_out, fact_left, fact_right, lambda n: fact_sem.at[n], place)

    def next_copies():
        return (send(fact_out, fact_next, next_sem.at[0], next_sem.at[1], place - 1, 0),)

    def start_copies():
        return pair(start_out, start_left, start_right, lambda n: start_sem.at[n], place)

    def fix_copies(piece):
        return pair(
            fix_out.at[piece],
            fix_left.at[piece],
            fix_right.at[piece],
            lambda n: fix_sem.at[n, piece],
            place,
        )

    def wave_copies(sweep, piece):
        flow_at = downstream[sweep]
        main = send(
            main_out.at[sweep, piece],
            main_in.at[sweep, piece],
            main_sem.at[0, sweep, piece],
            main_sem.at[1, sweep, piece],
            flow_at,
            0,
        )
        low = near_out.at[sweep, piece, pl.ds(0, NEAR)]
        high = near_out.at[sweep, piece, pl.ds(FACE, NEAR)]
        ahead, back = (low, high) if sweep == 0 else (high, low)
        near = (
            send(
                ahead,
                near_left.at[sweep, piece],
                near_sem.at[0, sweep, piece],
                near_sem.at[1, sweep, piece],
                flow_at,
                1,
            ),
            send(
                back,
                near_right.at[sweep, piece],
                near_sem.at[2, sweep, piece],
                near_sem.at[3, sweep, piece],
                flow_at,
                -1,
            ),
        )
        far = pair(
            near_out.at[sweep, piece, pl.ds(FACE if sweep == 0 else 3 * FACE, FACE)],
            far_left.at[sweep, piece],
            far_right.at[sweep, piece],
            lambda n: far_sem.at[n, sweep, piece],
            flow_at,
            2,
        )
        return far + near + (main,)

    pl.semaphore_wait(barrier, met)

    start_all(fact_copies())

    @pl.when(below)
    def _():
        start_all(next_copies())

    for fetch in fetches[4:]:
        fetch.wait()

    inverse = local_inverse[...]
    lifts = lift_rows[...].T
    trace = trace_rows[...]
    traced_inverse = jnp.dot(trace, inverse, precision=HIGH, preferred_element_type=F32)
    traced_lift = jnp.dot(trace, lifts, precision=HIGH, preferred_element_type=F32)
    widened(jnp.concatenate([inverse, traced_inverse], axis=0), wide, local_weight.at[0])
    widened(jnp.concatenate([inverse.T, lift_rows[...]], axis=0), wide, local_weight.at[1])
    widened(traced_lift, wide, chain_weight.at[0])
    widened(traced_lift.T, wide, chain_weight.at[1])
    widened(lifts, wide, out_weight.at[0])
    widened(traced_inverse.T, wide, out_weight.at[1])

    def one_hot(row, depth):
        rows = lax.broadcasted_iota(jnp.int32, (depth, TILE), 0)
        return jnp.where(rows == row, 1.0, 0.0).astype(BF16)

    def build_pick(piece, carry):
        for level in range(LEVELS_HERE):
            code = codes(level, piece)
            for at in range(GROUP):
                link = code[:, at * TILE : (at + 1) * TILE]
                row = jnp.where(
                    link < HALO,
                    link + (TILE + at * HALO),
                    jnp.where(
                        link < HALO + TILE, link - HALO, link + (HALF + at * HALO - HALO)
                    ),
                )
                row = jnp.where(link >= 0, row, -1)
                pick[level, piece * GROUP + at] = one_hot(row, 2 * TILE)
        return carry

    lax.fori_loop(0, pieces, build_pick, 0)

    def settle_facts():
        wait_received(fact_copies())

        @pl.when(above)
        def _():
            wait_received(next_copies())

        @pl.when(jnp.logical_not(above))
        def _():
            fact_next[...] = jnp.zeros(fact_next.shape, F32)

        lane = lanes(1)
        start = lax.rem(lane, HALF) // HALO * HALO
        on_left = lane < HALF

        def one(piece, carry):
            facts = inward(fact_left[piece], fact_right[piece])
            scale[0, piece, :, width:whole_width] = facts[0:1]
            link = facts[1:2].astype(jnp.int32)
            low = (link >= 0) & (link < HALO)
            high = link >= HALO + TILE
            after = link - (HALO + TILE)
            left_row = jnp.where(
                high, HALF + start + after, jnp.where(low, TILE + start + link, -1)
            )
            right_row = jnp.where(
                low, start + link, jnp.where(high, TILE + HALF + start + after, -1)
            )
            pick_beside[piece] = one_hot(jnp.where(on_left, left_row, right_row), 2 * TILE)
            link = fact_next[piece][1:2].astype(jnp.int32)
            inside = (link >= HALO) & (link < HALO + TILE)
            row = jnp.where(inside, start * (TILE // HALO) + link - HALO, -1)
            pick_next[piece] = one_hot(row, width)
            return carry

        lax.fori_loop(0, pieces, one, 0)

    def prepare(sweep):
        loaded(sweep).wait()

        def one(level, piece):
            cols = columns_of(piece)
            value = product(local_weight[sweep], stacked(results[sweep][level, :, cols]))
            mask = live(level, piece)
            results[sweep][level, :, cols] = mask * value[:nodes]
            added = (mask if sweep == 0 else scale[level, piece, :, 0:width]) * value[nodes:]
            lead[sweep, level, piece, :, 0:width] = added
            if level == 0:
                lead[sweep, 0, piece, :, width:whole_width] = jnp.zeros((BOTH, TILE), F32)
                if sweep == 0:
                    start_out[piece] = packed(added[FACE:])

        def first_level(piece, carry):
            one(0, piece)
            return carry

        def second_level(piece, carry):
            one(1, piece)
            return carry

        lax.fori_loop(0, pieces, first_level, 0)
        if sweep == 0:
            start_all(start_copies())
        lax.fori_loop(0, pieces, second_level, 0)

    def arrive(sweep, piece):
        @pl.when(is_first[sweep])
        def _():
            main_in[sweep, piece] = jnp.zeros((BOTH, width), F32)
            near_left[sweep, piece] = jnp.zeros((NEAR, TILE), F32)
            near_right[sweep, piece] = jnp.zeros((NEAR, TILE), F32)
            far_left[sweep, piece] = jnp.zeros((FACE, TILE), F32)
            far_right[sweep, piece] = jnp.zeros((FACE, TILE), F32)

        @pl.when(jnp.logical_not(is_first[sweep]))
        def _():
            wait_received(wave_copies(sweep, piece))

    def leave_far(sweep, piece):
        start_all(wave_copies(sweep, piece)[:2])

    def leave_near(sweep, piece):
        start_all(wave_copies(sweep, piece)[2:4])

    def leave(sweep, piece):
        start_all(wave_copies(sweep, piece)[4:])

    def picked(near, beyond, one_hots):
        near_high, near_low = near
        beyond_high, beyond_low = beyond
        extended = jnp.concatenate(
            [
                jnp.concatenate([near_high, beyond_high], axis=1),
                jnp.concatenate([near_low, beyond_low], axis=1),
            ],
            axis=0,
        )
        value = product(extended, one_hots)
        return value[:FACE] + value[FACE:]

    def spread(value, one_hots):
        value = cross_product(jnp.concatenate(halves(value), axis=0), one_hots)
        return value[:FACE] + value[FACE:]

    def cut(value, at):
        return value[:, at * TILE : (at + 1) * TILE]

    def gathered(sides, halo, level, piece):
        halo = halves(halo)
        high, low = halves(sides)
        return [
            picked((cut(high, at), cut(low, at)), halo, pick[level, piece * GROUP + at])
            for at in range(GROUP)
        ]

    def scattered(sides, level, piece):
        own = []
        edge = jnp.zeros((FACE, TILE), F32)
        for at in range(GROUP):
            value = spread(cut(sides, at), pick[level, piece * GROUP + at])
            own.append(value[:, :TILE])
            edge = edge + value[:, TILE:]
        return own, edge

    def forward(piece):
        arrive(0, piece)
        main = main_in[0, piece]
        near = inward(*unfolded(near_left[0, piece], near_right[0, piece]))
        outer = inward(far_left[0, piece], far_right[0, piece], 2)
        sides = gathered(main[FACE:], near[BOTH:], 0, piece)
        sides.append(
            near[FACE:BOTH]
            + picked(halves(packed(main[FACE:])), halves(outer), pick_beside[piece])
        )
        inbound = jnp.concatenate(
            [
                jnp.concatenate([main[:FACE], near[:FACE]], axis=1),
                jnp.concatenate(sides, axis=1),
            ],
            axis=0,
        )
        operand = stacked(inbound)
        kept[0, 0, piece] = operand[:, :width]
        value = lead[0, 0, piece] + scale[0, piece] * product(chain_weight[0], operand)
        sides = gathered(value[FACE:, :width], value[FACE:, width:], 1, piece)
        operand = stacked(
            jnp.concatenate([value[:FACE, :width], jnp.concatenate(sides, axis=1)], axis=0)
        )
        kept[0, 1, piece] = operand

        @pl.when(jnp.logical_not(is_last[0]))
        def _():
            value = lead[0, 1, piece, :, 0:width] + scale[1, piece, :, 0:width] * product(
                chain_weight[0], operand
            )
            edges = packed(value)
            near_out[0, piece, FACE : 2 * FACE] = edges[FACE:]
            leave_far(0, piece)
            ahead = product(jnp.concatenate(halves(value[FACE:]), axis=0), pick_next[piece])
            low, high = folded(edges[:FACE], ahead[:FACE] + ahead[FACE:])
            near_out[0, piece, 0:FACE] = low
            near_out[0, piece, 2 * FACE : 3 * FACE] = high
            leave_near(0, piece)
            main_out[0, piece] = value
            leave(0, piece)

    def adjoint(piece):
        arrive(1, piece)
        main = main_in[1, piece]
        highs, lows = near_left[1, piece], near_right[1, piece]
        near = homeward(*unfolded(lows, highs)[::-1])
        outer = homeward(far_left[1, piece], far_right[1, piece], 2)
        edges = jnp.concatenate(
            [near[:FACE], near[BOTH:] + outer], axis=0
        )
        behind = spread(near[FACE:BOTH], pick_next[piece])
        none = jnp.zeros((FACE, TILE), F32)
        inbound = jnp.concatenate(
            [
                cut(main, at)
                + unpacked(edges, at)
                + jnp.concatenate([none, cut(behind, at)], axis=0)
                for at in range(GROUP)
            ],
            axis=1,
        )
        operand = stacked(inbound)
        kept[1, 1, piece] = operand
        value = lead[1, 1, piece, :, 0:width] + scale[1, piece, :, 0:width] * product(
            chain_weight[1], operand
        )
        own, edge = scattered(value[FACE:], 1, piece)
        fix_out[piece] = edge
        inbound = jnp.concatenate(
            [
                jnp.concatenate([value[:FACE], none], axis=1),
                jnp.concatenate(own + [edge], axis=1),
            ],
            axis=0,
        )
        late[piece] = inbound[:, :width]

        @pl.when(jnp.logical_not(is_last[1]))
        def _():
            value = lead[1, 0, piece] + scale[0, piece] * product(
                chain_weight[1], stacked(inbound)
            )
            around = spread(value[FACE:, width:], pick_beside[piece])
            near_out[1, piece, 3 * FACE : 4 * FACE] = around[:, TILE:]
            leave_far(1, piece)
            own, edge = scattered(value[FACE:, :width], 0, piece)
            low, high = folded(value[:FACE, width:], value[FACE:, width:])
            near_out[1, piece, 0:FACE] = low
            near_out[1, piece, FACE : 2 * FACE] = edge
            near_out[1, piece, 2 * FACE : 3 * FACE] = high
            leave_near(1, piece)
            own = [own[at] + unpacked(around[:, :TILE], at) for at in range(GROUP)]
            main_out[1, piece, 0:FACE] = value[:FACE, :width]
            main_out[1, piece, FACE:BOTH] = jnp.concatenate(own, axis=1)
            leave(1, piece)

        start_all(fix_copies(piece))

    def finish(sweep, level, piece):
        cols = columns_of(piece)
        if sweep == 1 and level == 0:
            wait_received(fix_copies(piece))
            edges = homeward(fix_left[piece], fix_right[piece])
            sides = [
                cut(late[piece, FACE:BOTH], at) + unpacked(edges, at) for at in range(GROUP)
            ]
            operand = stacked(
                jnp.concatenate([late[piece, 0:FACE], jnp.concatenate(sides, axis=1)], axis=0)
            )
        else:
            operand = kept[sweep, level, piece]
        factor = scale[level, piece, :, 0:width] if sweep == 0 else live(level, piece)
        results[sweep][level, :, cols] += factor * product(out_weight[sweep], operand)

    def chain(sweep):
        step = forward if sweep == 0 else adjoint
        if sweep == 0:
            wait_received(start_copies())

            def begin(piece, carry):
                lead[0, 0, piece, FACE:BOTH, width:whole_width] = inward(
                    start_left[piece], start_right[piece]
                )
                return carry

            lax.fori_loop(0, pieces, begin, 0)

        def one(piece, carry):
            step(piece)
            return carry

        def upper(piece, carry):
            finish(sweep, 1, piece)
            return carry

        def last(piece, carry):
            finish(sweep, 0, piece)
            return carry

        lax.fori_loop(0, pieces, one, 0)
        lax.fori_loop(0, pieces, upper, 0)
        lax.fori_loop(0, pieces, last, 0)

    first = (place >= flow_count // 2).astype(jnp.int32)
    on_end = jnp.logical_or(place == 0, place == flow_count - 1)

    def slot(at, carry):
        early = jnp.where(on_end, 2 + first, 1 - first)
        late_op = jnp.where(on_end, 1 - first, 2 + first)
        op = jnp.where(
            at == 0, first, jnp.where(at == 1, early, jnp.where(at == 2, late_op, 3 - first))
        )

        @pl.when(op == 0)
        def _():
            prepare(0)

        @pl.when(op == 1)
        def _():
            prepare(1)

        @pl.when(at == 0)
        def _():
            settle_facts()

        @pl.when(op == 2)
        def _():
            chain(0)

        @pl.when(op == 3)
        def _():
            chain(1)

        return carry

    lax.fori_loop(0, 4, slot, 0)

    wait_sent(fact_copies() + start_copies())

    @pl.when(below)
    def _():
        wait_sent(next_copies())

    def settle(piece, carry):
        wait_sent(fix_copies(piece))
        for sweep in range(2):
            @pl.when(jnp.logical_not(is_last[sweep]))
            def _():
                wait_sent(wave_copies(sweep, piece))

        return carry

    lax.fori_loop(0, pieces, settle, 0)


def per_device(
    source,
    cotangent,
    flux,
    pore_mask,
    upwind,
    side_link,
    local_inverse,
    flow_lift,
    side_lift,
    flow_trace,
    side_trace,
):
    levels, nodes, elems = source.shape
    tiles = elems // TILE
    pieces = tiles // GROUP
    width = GROUP * TILE
    extended = width + TILE
    away = pl.BlockSpec(memory_space=pltpu.HBM)
    here = pl.BlockSpec(memory_space=pltpu.VMEM)
    dma = pltpu.SemaphoreType.DMA
    return pl.pallas_call(
        kernel,
        out_shape=(
            pltpu.VMEM(source.shape, F32),
            pltpu.VMEM(source.shape, F32),
        ),
        in_specs=[away] * 11,
        out_specs=(here, here),
        scratch_shapes=[
            pltpu.VMEM((2, levels, pieces, BOTH, extended), F32),
            pltpu.VMEM((levels, pieces, 1, extended), F32),
            pltpu.VMEM((levels, tiles, 2 * TILE, TILE), BF16),
            pltpu.VMEM((pieces, 2 * TILE, TILE), BF16),
            pltpu.VMEM((pieces, width, TILE), BF16),
            pltpu.VMEM((2, levels, pieces, 3 * BOTH, width), BF16),
            pltpu.VMEM((pieces, BOTH, width), F32),
            pltpu.VMEM((2, pieces, BOTH, width), F32),
            pltpu.VMEM((2, pieces, BOTH, width), F32),
            pltpu.VMEM((2, pieces, 4 * FACE, TILE), F32),
            pltpu.VMEM((2, pieces, NEAR, TILE), F32),
            pltpu.VMEM((2, pieces, NEAR, TILE), F32),
            pltpu.VMEM((2, pieces, FACE, TILE), F32),
            pltpu.VMEM((2, pieces, FACE, TILE), F32),
            pltpu.VMEM((pieces, FACE, TILE), F32),
            pltpu.VMEM((pieces, FACE, TILE), F32),
            pltpu.VMEM((pieces, FACE, TILE), F32),
            pltpu.VMEM((pieces, 8, TILE), F32),
            pltpu.VMEM((pieces, 8, TILE), F32),
            pltpu.VMEM((pieces, 8, TILE), F32),
            pltpu.VMEM((pieces, 8, TILE), F32),
            pltpu.VMEM((pieces, FACE, TILE), F32),
            pltpu.VMEM((pieces, FACE, TILE), F32),
            pltpu.VMEM((pieces, FACE, TILE), F32),
            pltpu.VMEM((levels, elems), F32),
            pltpu.VMEM((levels, elems), jnp.int32),
            pltpu.VMEM((levels, elems), jnp.int32),
            pltpu.VMEM((levels, elems), jnp.int32),
            pltpu.VMEM((nodes, nodes), F32),
            pltpu.VMEM((BOTH, nodes), F32),
            pltpu.VMEM((BOTH, nodes), F32),
            pltpu.VMEM((nodes + BOTH, 3 * nodes), F32),
            pltpu.VMEM((2, nodes + BOTH, 3 * nodes), BF16),
            pltpu.VMEM((2, BOTH, 3 * BOTH), BF16),
            pltpu.VMEM((2, nodes, 3 * BOTH), BF16),
            dma((9,)),
            dma((2,)),
            dma((2, 2, pieces)),
            dma((4, 2, pieces)),
            dma((4, 2, pieces)),
            dma((4, pieces)),
            dma((4,)),
            dma((2,)),
            dma((4,)),
        ],
        compiler_params=pltpu.CompilerParams(
            collective_id=0, has_side_effects=True, vmem_limit_bytes=LIMIT << 20
        ),
    )(
        *(
            pltpu.with_memory_space_constraint(operand, pltpu.HBM)
            for operand in (
                source,
                cotangent,
                flux,
                pore_mask,
                upwind,
                side_link,
                local_inverse,
                flow_lift.T,
                side_lift.T,
                flow_trace,
                side_trace,
            )
        )
    )


def solution(mesh):
    placed = (
        P("flow", None, "cross"),
        P("flow", None, "cross"),
        P("flow", "cross"),
        P("flow", "cross"),
        P("flow", "cross"),
        P("flow", "cross"),
        P(),
        P(),
        P(),
        P(),
        P(),
    )
    return jax.shard_map(
        per_device,
        mesh=mesh,
        in_specs=placed,
        out_specs=(P("flow", None, "cross"), P("flow", None, "cross")),
        check_vma=False,
    )
```
